512 devices in a mesh: date: 16 (over z, y_lo), az: 32 (over y_hi, x, core).
Axes of the slice: x: 4, y: 8 (y_hi: 4, y_lo: 2; y = y_hi * 2 + y_lo), z: 8, core: 2. Of those that a mesh axis runs over, the one named last changes fastest.
Arguments:
- slc_stack: bfloat16 [2, 256, 4096, 128], P(None, 'date', 'az'), may hold values from -6 to 6
- fir_taps: float32 [256, 5], P('date'), may hold values from 0.1 to 1
- look_index: int32 [32, 16, 64], P('az', 'date'), may hold values from 0 to 1023
- shrink_level: int32 [32, 16], P('az', 'date'), may hold values from 1 to 12
- window_half: int32 [256], replicated, may hold values from 0 to 2
- basis: bfloat16 [32, 256], replicated, may hold values from -0.375 to 0.375
Outputs:
- projection: float32 [32, 2, 4096, 128], P('date', None, 'az')
The draws below stay inside these ranges and needn't reach their ends.
Inputs may be any that keep to these rules, and one draw needn't show every extreme that they name: `look_index`: pixel numbers inside one block of 8 rows.
All inputs are finite; a program needn't handle non-finite values.
Results may differ from the reference program's by a relative error of at most 0.0048.
Values may be sent and summed in bfloat16 or wider, within the bound.
No kernel may reach another device: no remote copies, remote signals or barrier semaphores. Data moves between devices by JAX's collectives and lax.ppermute only.
A program may use at most 64 MiB of HBM per device.

```python
import jax
import jax.numpy as jnp
from jax import lax

DATES = 256
BASES = 32
LOOKS = 64
NS_ITERS = 6
FIR_REACH = 2
SMOOTH_REACH = 2
RG = 128
PIX_DEV = 1024
TAPS = 5
BLOCK_ROWS = 8
AZ = 4096
N_DATE = 16
N_AZ = 32


def touch_ends(entries, rng, least, largest):
    place = [jax.random.randint(jax.random.fold_in(rng, axis), (), 0, length) for axis, length in enumerate(entries.shape)]
    main_axis = entries.shape.index(max(entries.shape))
    neighbour = place[:main_axis] + [(place[main_axis] + 1) % entries.shape[main_axis]] + place[main_axis + 1:]
    return entries.at[tuple(place)].set(least).at[tuple(neighbour)].set(largest)


def shard_levels(rng, extent, split, smallest, top_value):
    level = 1.0
    for dim, blocks in split:
        steps = jax.random.uniform(jax.random.fold_in(jax.random.fold_in(rng, 6), dim), (blocks,), jnp.float32, smallest / len(split), top_value / len(split))
        level = level * jnp.repeat(jnp.exp(steps), extent[dim] // blocks).reshape((-1,) + (1,) * (len(extent) - 1 - dim))
    return level


def normal_values(rng, shape, width, most, split=(), held_as=jnp.bfloat16):
    level = shard_levels(rng, shape, split, -0.22, 0.18) if split else 1.0
    values = jax.random.normal(rng, shape, jnp.float32) * width * level
    return jnp.minimum(jnp.maximum(values, -most), most).astype(held_as)


def setup_inputs(seed: int = 0) -> dict:
    seeds = jax.random.split(jax.random.key(seed), 7)
    slc_stack = normal_values(seeds[0], (2, DATES, AZ, RG), 1.0, 6.0, ((1, 16), (2, 32)))
    fir_taps = jnp.clip(0.1 + 0.9 * jax.random.uniform(seeds[1], (DATES, TAPS), jnp.float32) ** shard_levels(seeds[1], (DATES, TAPS), ((0, 16),), -0.2, 0.2), 0.1, 1.0)
    look_index = touch_ends(jax.random.randint(seeds[2], (N_AZ, N_DATE, LOOKS), 0, PIX_DEV), jax.random.fold_in(seeds[2], 1), 0, PIX_DEV - 1).astype(jnp.int32)
    shrink_level = touch_ends(jax.random.randint(seeds[3], (N_AZ, N_DATE), 1, 13), jax.random.fold_in(seeds[3], 1), 1, 12).astype(jnp.int32)
    window_half = touch_ends(jax.random.randint(seeds[4], (DATES,), 0, SMOOTH_REACH + 1), jax.random.fold_in(seeds[4], 1), 0, SMOOTH_REACH).astype(jnp.int32)
    basis = normal_values(seeds[5], (BASES, DATES), DATES ** -0.5, 0.375)
    return dict(slc_stack=slc_stack, fir_taps=fir_taps, look_index=look_index, shrink_level=shrink_level, window_half=window_half, basis=basis)


def complex_product(left_re, left_im, right_re, right_im):
    highest = lax.Precision.HIGHEST
    real = jnp.dot(left_re, right_re, precision=highest) - jnp.dot(left_im, right_im, precision=highest)
    imag = jnp.dot(left_re, right_im, precision=highest) + jnp.dot(left_im, right_re, precision=highest)
    return (real, imag)

def wiener_block(pixels, chosen, level):
    sample = jnp.take(pixels, chosen, axis=2)
    samp_re = sample[0]
    samp_im = sample[1]
    looks = chosen.shape[0]
    gram_re = (jnp.dot(samp_re, samp_re.T, preferred_element_type=jnp.float32) + jnp.dot(samp_im, samp_im.T, preferred_element_type=jnp.float32)) / looks
    gram_im = (jnp.dot(samp_im, samp_re.T, preferred_element_type=jnp.float32) - jnp.dot(samp_re, samp_im.T, preferred_element_type=jnp.float32)) / looks
    count = gram_re.shape[0]
    identity = jnp.eye(count, dtype=jnp.float32)
    level_mean = jnp.trace(gram_re) / count + 1e-06
    weight = level.astype(jnp.float32) / 16.0
    shrunk_re = (1.0 - weight) * gram_re + weight * level_mean * identity
    shrunk_im = (1.0 - weight) * gram_im
    load_re = shrunk_re + level_mean * identity
    load_im = shrunk_im
    scale = 1.0 / jnp.sqrt(jnp.sum(load_re * load_re + load_im * load_im))
    inv_re = identity * scale
    inv_im = jnp.zeros_like(identity)
    for step in range(NS_ITERS):
        prod_re, prod_im = complex_product(load_re, load_im, inv_re, inv_im)
        inv_re, inv_im = complex_product(inv_re, inv_im, 2.0 * identity - prod_re, -prod_im)
    gain_re, gain_im = complex_product(shrunk_re, shrunk_im, inv_re, inv_im)
    gain_re = gain_re.astype(jnp.bfloat16)
    gain_im = gain_im.astype(jnp.bfloat16)
    pix_re = pixels[0]
    pix_im = pixels[1]
    out_re = jnp.dot(gain_re, pix_re, preferred_element_type=jnp.float32) - jnp.dot(gain_im, pix_im, preferred_element_type=jnp.float32)
    out_im = jnp.dot(gain_re, pix_im, preferred_element_type=jnp.float32) + jnp.dot(gain_im, pix_re, preferred_element_type=jnp.float32)
    return jnp.stack([out_re, out_im]).astype(jnp.bfloat16)

def smooth_weights(halves, reach):
    offsets = jnp.arange(-reach, reach + 1)
    inside = (jnp.abs(offsets)[None, :] <= halves[:, None]).astype(jnp.float32)
    return inside / (2 * halves + 1).astype(jnp.float32)[:, None]

def reference(slc_stack, fir_taps, look_index, shrink_level, window_half, basis):
    rows = slc_stack.shape[2]
    padded = jnp.pad(slc_stack.astype(jnp.float32), ((0, 0), (0, 0), (FIR_REACH, FIR_REACH), (0, 0)))
    filtered = jnp.zeros(slc_stack.shape, jnp.float32)
    for offset in range(TAPS):
        filtered = filtered + fir_taps[:, offset][None, :, None, None] * padded[:, :, offset:offset + rows, :]
    filtered = filtered.astype(jnp.bfloat16)
    blocks = rows // BLOCK_ROWS
    grouped = filtered.reshape(2, DATES, blocks, PIX_DEV).transpose(2, 0, 1, 3)
    chosen_all = look_index.reshape(blocks, LOOKS).astype(jnp.int32)
    levels = shrink_level.reshape(blocks).astype(jnp.int32)
    wiener = lax.map(lambda item: wiener_block(item[0], item[1], item[2]), (grouped, chosen_all, levels))
    wiener = wiener.transpose(1, 2, 0, 3).reshape(2, DATES, rows, RG)
    weights = smooth_weights(window_half, SMOOTH_REACH)
    rim = jnp.pad(wiener.astype(jnp.float32), ((0, 0), (0, 0), (SMOOTH_REACH, SMOOTH_REACH), (0, 0)))
    smoothed = jnp.zeros(wiener.shape, jnp.float32)
    for offset in range(2 * SMOOTH_REACH + 1):
        smoothed = smoothed + weights[:, offset][None, :, None, None] * rim[:, :, offset:offset + rows, :]
    smoothed = smoothed.astype(jnp.bfloat16)
    return jnp.einsum('kt,ctrg->kcrg', basis.astype(jnp.float32), smoothed.astype(jnp.float32), precision=lax.Precision.HIGHEST)
```

```python
import functools

import jax
import jax.numpy as jnp
from jax import lax
from jax.experimental import pallas as pl
from jax.experimental.pallas import tpu as pltpu
from jax.sharding import PartitionSpec as P

NS_ITERS = 6
REACH = 2
INTERPRET = False


def filter_kernel(slc_ref, low_ref, high_ref, taps_ref, out_ref, held):
    _, dates, rows, cols = slc_ref.shape
    blocks = out_ref.shape[0]
    block_rows = rows // blocks
    pitch = held.shape[0] // dates
    taps = [
        jnp.broadcast_to(taps_ref[:, j : j + 1], (dates, cols)) for j in range(2 * REACH + 1)
    ]
    for c in range(2):
        for t in range(dates):
            held[pl.ds(t * pitch, rows), :] = slc_ref[c, t].astype(jnp.float32)

        def line(r):
            if r < 0:
                return low_ref[c, r + REACH].astype(jnp.float32)
            if r >= rows:
                return high_ref[c, r - rows].astype(jnp.float32)
            return held[pl.ds(r, dates, stride=pitch), :]

        window = [line(r) for r in range(-REACH, REACH)]
        for r in range(rows):
            window.append(line(r + REACH))
            total = taps[0] * window[0]
            for j in range(1, 2 * REACH + 1):
                total = total + taps[j] * window[j]
            window.pop(0)
            b, i = divmod(r, block_rows)
            out_ref[b, c, :, i * cols : (i + 1) * cols] = total.astype(jnp.bfloat16)


def split(x):
    hi = x.astype(jnp.bfloat16)
    return hi, (x - hi.astype(jnp.float32)).astype(jnp.bfloat16)


def dot(a, b):
    return jnp.dot(a, b, preferred_element_type=jnp.float32)


def dot3(a, b):
    a_hi, a_lo = split(a)
    b_hi, b_lo = split(b)
    return dot(
        jnp.concatenate([a_hi, a_lo, a_hi], 1), jnp.concatenate([b_hi, b_hi, b_lo], 0)
    )


def total(x):
    return jnp.sum(jnp.sum(x, axis=1, keepdims=True), axis=0, keepdims=True)


def link_kernel(pix_ref, look_ref, level_ref, half_ref, basis_ref, out_ref, stage):
    groups, _, dates_own, pixels = pix_ref.shape
    dates = groups * dates_own
    looks = look_ref.shape[1] // 2
    cols = stage.shape[2]
    block_rows = pixels // cols
    z = jnp.concatenate(
        [pix_ref[:, c].reshape(dates, pixels) for c in range(2)], axis=0
    )
    place = lax.broadcasted_iota(jnp.int32, (pixels, 2 * looks), 0)
    picked = (place == look_ref[...]).astype(jnp.float32).astype(jnp.bfloat16)
    samples = dot(z, picked)
    first = lax.broadcasted_iota(jnp.int32, (dates, 2 * looks), 1) < looks
    samp_re = samples[:dates]
    samp_im = samples[dates:]
    tall = jnp.concatenate(
        [jnp.where(first, samp_re, -samp_im), jnp.where(first, samp_im, samp_re)], 0
    )
    wide = tall.T.astype(jnp.bfloat16)
    tall = tall.astype(jnp.bfloat16)
    inner = dot(wide, tall)

    width = 2 * looks
    rows_i = lax.broadcasted_iota(jnp.int32, (width, width), 0)
    cols_i = lax.broadcasted_iota(jnp.int32, (width, width), 1)
    identity = (rows_i == cols_i).astype(jnp.float32)
    trace = total(inner * identity) * 0.5
    square = total(inner * inner) * 0.5
    mean = trace / (looks * dates) + 1e-06
    weight = level_ref[...].astype(jnp.float32) / 16.0
    alpha = weight * mean + mean
    beta = (1.0 - weight) / looks
    scale = 1.0 / jnp.sqrt(
        dates * alpha * alpha + 2.0 * alpha * beta * trace + beta * beta * square
    )

    t = scale * alpha
    x = jnp.ones_like(t)
    w = (scale * beta) * inner
    m = (2.0 - 2.0 * t) * identity - w
    u = -identity
    w = (2.0 - 2.0 * t) * w - dot3(w, w)
    x, t = x * (2.0 - t), 2.0 * t - t * t
    for step in range(1, NS_ITERS):
        last = step == NS_ITERS - 1
        stack = [m, u] if last else [m, u, w]
        prod = dot3(jnp.concatenate(stack, 0), w)
        m, u = (
            (2.0 - 2.0 * t) * m - prod[:width],
            (2.0 - t) * u - x * m - prod[width : 2 * width],
        )
        if not last:
            w = (2.0 - 2.0 * t) * w - prod[2 * width :]
        x, t = x * (2.0 - t), 2.0 * t - t * t

    half = half_ref[...]
    share = basis_ref[...].astype(jnp.float32) / (2 * half + 1).astype(jnp.float32)
    near = jnp.concatenate(
        [jnp.where(half >= j, share, 0.0) for j in range(REACH + 1)], axis=0
    )
    near_hi, near_lo = split(near)
    seen = [
        dot(near_hi, tall[c * dates : (c + 1) * dates])
        + dot(near_lo, tall[c * dates : (c + 1) * dates])
        for c in range(2)
    ]
    core = dot3(jnp.concatenate(seen, 0), (scale * beta) * (m - (mean * scale) * u))
    plain = (t - mean * scale * x) * near
    nothing = jnp.zeros_like(plain)
    core_hi, core_lo = split(core)
    gain = (
        dot(core_hi, wide)
        + dot(core_lo, wide)
        + jnp.concatenate(
            [
                jnp.concatenate([plain, nothing], 1),
                jnp.concatenate([nothing, plain], 1),
            ],
            0,
        )
    )
    proj = dot(gain.astype(jnp.bfloat16), z)

    bases = basis_ref.shape[0]
    taps = 2 * bases * (REACH + 1) // 2

    def part(c, j, row):
        start = c * taps + abs(j) * bases
        return proj[start : start + bases, row * cols : (row + 1) * cols]

    def smoothed(c, row):
        out = None
        for j in range(-REACH, REACH + 1):
            if 0 <= row + j < block_rows:
                term = part(c, j, row + j)
                out = term if out is None else out + term
        return out

    below = [block_rows, block_rows + 1]
    above = [-2, -1]
    slots = [(0, r) for r in range(block_rows)] + [(1, r) for r in range(block_rows)]
    slots += [(0, r) for r in below] + [(1, r) for r in below]
    slots += [(1, r) for r in above] + [(0, r) for r in above]
    for q, (c, row) in enumerate(slots):
        stage[q] = smoothed(c, row)
    flat = stage.reshape(len(slots) * bases, cols)
    own = bases // groups
    for d in range(groups):
        lines = [
            [
                flat[pl.ds(q * block_rows * bases + d * own + k, block_rows, stride=bases), :]
                for q in range(3)
            ]
            for k in range(own)
        ]
        rows = [v for k in range(own) for v in lines[k][:2]] + [lines[k][2] for k in range(own)]
        out_ref[d] = jnp.concatenate(rows, 0).astype(jnp.bfloat16)


def join_kernel(part_ref, low_ref, high_ref, out_ref):
    groups = part_ref.shape[0]
    own, _, rows, cols = out_ref.shape
    block_rows = rows // groups
    sub = lax.broadcasted_iota(jnp.int32, (block_rows, cols), 0)

    def lent(ref_value, k):
        start = k * block_rows
        return ref_value[start : start + block_rows].astype(jnp.float32)

    base = own * 2 * block_rows
    for k in range(own):
        lends = (
            [lent(low_ref[...], k)]
            + [lent(part_ref[b, base:, :], k) for b in range(groups)]
            + [lent(high_ref[...], k)]
        )
        for b in range(groups):
            for c in range(2):
                start = (k * 2 + c) * block_rows
                main = part_ref[b, start : start + block_rows, :].astype(jnp.float32)
                before = lends[b]
                after = lends[b + 2]
                if c == 1:
                    before = pltpu.roll(before, block_rows - 2, 0)
                    after = pltpu.roll(after, 2, 0)
                out_ref[k, c, b * block_rows : (b + 1) * block_rows, :] = (
                    main
                    + jnp.where(sub < 2, before, 0.0)
                    + jnp.where(sub >= block_rows - 2, after, 0.0)
                )


def vmem(count):
    return [pl.BlockSpec(memory_space=pltpu.VMEM)] * count


def shifts(axis):
    count = lax.axis_size(axis)
    forward = [(i, i + 1) for i in range(count - 1)]
    return forward, [(b, a) for a, b in forward]


def on_device(slc_stack, fir_taps, look_index, shrink_level, window_half, basis):
    date_local, rows, cols = slc_stack.shape[1:]
    groups = lax.axis_size("date")
    block_rows = rows // groups
    pixels = block_rows * cols
    bases, dates = basis.shape
    own = bases // groups
    forward, backward = shifts("az")

    edge_low = jnp.swapaxes(slc_stack[:, :, rows - REACH :, :], 1, 2)
    edge_high = jnp.swapaxes(slc_stack[:, :, :REACH, :], 1, 2)
    low = lax.ppermute(edge_low, "az", forward)
    high = lax.ppermute(edge_high, "az", backward)
    pitch = rows + 8
    blocks = pl.pallas_call(
        filter_kernel,
        out_shape=jax.ShapeDtypeStruct((groups, 2, date_local, pixels), jnp.bfloat16),
        in_specs=vmem(4),
        out_specs=vmem(1)[0],
        scratch_shapes=[pltpu.VMEM((date_local * pitch, cols), jnp.float32)],
        interpret=INTERPRET,
        name="azimuth_filter",
    )(slc_stack, low, high, fir_taps)
    pix = lax.all_to_all(blocks, "date", split_axis=0, concat_axis=0, tiled=True)

    look = look_index.reshape(1, -1)
    slots = 3 * block_rows
    height = 3 * own * block_rows
    lent = pl.pallas_call(
        link_kernel,
        out_shape=jax.ShapeDtypeStruct((groups, height, cols), jnp.bfloat16),
        in_specs=vmem(5),
        out_specs=vmem(1)[0],
        scratch_shapes=[pltpu.VMEM((slots, bases, cols), jnp.float32)],
        interpret=INTERPRET,
        name="phase_link",
    )(
        pix,
        jnp.concatenate([look, look], 1),
        shrink_level,
        window_half.reshape(1, dates),
        basis,
    )
    parts = lax.all_to_all(lent, "date", split_axis=0, concat_axis=0, tiled=True)

    base = 2 * own * block_rows
    above = lax.ppermute(parts[0, base:, :], "az", backward)
    below = lax.ppermute(parts[groups - 1, base:, :], "az", forward)
    return pl.pallas_call(
        join_kernel,
        out_shape=jax.ShapeDtypeStruct((own, 2, rows, cols), jnp.float32),
        in_specs=vmem(3),
        out_specs=vmem(1)[0],
        interpret=INTERPRET,
        name="overlap_add",
    )(parts, below, above)


def solution(mesh):
    in_specs = (
        P(None, "date", "az", None),
        P("date", None),
        P("az", "date", None),
        P("az", "date"),
        P(),
        P(),
    )
    out_specs = P("date", None, "az", None)
    return jax.shard_map(
        on_device, mesh=mesh, in_specs=in_specs, out_specs=out_specs, check_vma=False
    )
```

```python
import functools

import jax
import jax.numpy as jnp
from jax import lax
from jax.experimental import pallas as pl
from jax.experimental.pallas import tpu as pltpu
from jax.sharding import PartitionSpec as P

NS_ITERS = 6
REACH = 2
INTERPRET = False


def filter_kernel(slc_ref, low_ref, high_ref, taps_ref, out_ref, held):
    _, dates, rows, cols = slc_ref.shape
    blocks = out_ref.shape[0]
    block_rows = rows // blocks
    pitch = held.shape[0] // dates
    taps = [
        jnp.broadcast_to(taps_ref[:, j : j + 1], (dates, cols)) for j in range(2 * REACH + 1)
    ]
    for c in range(2):
        for t in range(dates):
            held[pl.ds(t * pitch, rows), :] = slc_ref[c, t].astype(jnp.float32)

        def line(r):
            if r < 0:
                return low_ref[c, r + REACH].astype(jnp.float32)
            if r >= rows:
                return high_ref[c, r - rows].astype(jnp.float32)
            return held[pl.ds(r, dates, stride=pitch), :]

        window = [line(r) for r in range(-REACH, REACH)]
        for r in range(rows):
            window.append(line(r + REACH))
            total = taps[0] * window[0]
            for j in range(1, 2 * REACH + 1):
                total = total + taps[j] * window[j]
            window.pop(0)
            b, i = divmod(r, block_rows)
            out_ref[b, c, :, i * cols : (i + 1) * cols] = total.astype(jnp.bfloat16)


def split(x):
    hi = x.astype(jnp.bfloat16)
    return hi, (x - hi.astype(jnp.float32)).astype(jnp.bfloat16)


def dot(a, b):
    return jnp.dot(a, b, preferred_element_type=jnp.float32)


def dot3(a, b):
    a_hi, a_lo = split(a)
    b_hi, b_lo = split(b)
    return dot(
        jnp.concatenate([a_hi, a_lo, a_hi], 1), jnp.concatenate([b_hi, b_hi, b_lo], 0)
    )


def total(x):
    return jnp.sum(jnp.sum(x, axis=1, keepdims=True), axis=0, keepdims=True)


def link_kernel(pix_ref, look_ref, level_ref, half_ref, basis_ref, out_ref, stage):
    groups, _, dates_own, pixels = pix_ref.shape
    dates = groups * dates_own
    looks = look_ref.shape[1] // 2
    cols = stage.shape[2]
    block_rows = pixels // cols
    z = jnp.concatenate(
        [pix_ref[:, c].reshape(dates, pixels) for c in range(2)], axis=0
    )
    place = lax.broadcasted_iota(jnp.int32, (pixels, 2 * looks), 0)
    picked = (place == look_ref[...]).astype(jnp.float32).astype(jnp.bfloat16)
    samples = dot(z, picked)
    first = lax.broadcasted_iota(jnp.int32, (dates, 2 * looks), 1) < looks
    samp_re = samples[:dates]
    samp_im = samples[dates:]
    tall = jnp.concatenate(
        [jnp.where(first, samp_re, -samp_im), jnp.where(first, samp_im, samp_re)], 0
    )
    wide = tall.T.astype(jnp.bfloat16)
    tall = tall.astype(jnp.bfloat16)
    inner = dot(wide, tall)

    width = 2 * looks
    rows_i = lax.broadcasted_iota(jnp.int32, (width, width), 0)
    cols_i = lax.broadcasted_iota(jnp.int32, (width, width), 1)
    identity = (rows_i == cols_i).astype(jnp.float32)
    trace = total(inner * identity) * 0.5
    square = total(inner * inner) * 0.5
    mean = trace / (looks * dates) + 1e-06
    weight = level_ref[...].astype(jnp.float32) / 16.0
    alpha = weight * mean + mean
    beta = (1.0 - weight) / looks
    scale = 1.0 / jnp.sqrt(
        dates * alpha * alpha + 2.0 * alpha * beta * trace + beta * beta * square
    )

    t = scale * alpha
    x = jnp.ones_like(t)
    w = (scale * beta) * inner
    m = (2.0 - 2.0 * t) * identity - w
    u = -identity
    w = (2.0 - 2.0 * t) * w - dot3(w, w)
    x, t = x * (2.0 - t), 2.0 * t - t * t
    for step in range(1, NS_ITERS):
        last = step == NS_ITERS - 1
        stack = [m, u] if last else [m, u, w]
        prod = dot3(jnp.concatenate(stack, 0), w)
        m, u = (
            (2.0 - 2.0 * t) * m - prod[:width],
            (2.0 - t) * u - x * m - prod[width : 2 * width],
        )
        if not last:
            w = (2.0 - 2.0 * t) * w - prod[2 * width :]
        x, t = x * (2.0 - t), 2.0 * t - t * t

    half = half_ref[...]
    share = basis_ref[...].astype(jnp.float32) / (2 * half + 1).astype(jnp.float32)
    near = jnp.concatenate(
        [jnp.where(half >= j, share, 0.0) for j in range(REACH + 1)], axis=0
    )
    near_hi, near_lo = split(near)
    seen = [
        dot(near_hi, tall[c * dates : (c + 1) * dates])
        + dot(near_lo, tall[c * dates : (c + 1) * dates])
        for c in range(2)
    ]
    core = dot3(jnp.concatenate(seen, 0), (scale * beta) * (m - (mean * scale) * u))
    plain = (t - mean * scale * x) * near
    nothing = jnp.zeros_like(plain)
    core_hi, core_lo = split(core)
    gain = (
        dot(core_hi, wide)
        + dot(core_lo, wide)
        + jnp.concatenate(
            [
                jnp.concatenate([plain, nothing], 1),
                jnp.concatenate([nothing, plain], 1),
            ],
            0,
        )
    )
    proj = dot(gain.astype(jnp.bfloat16), z)

    bases = basis_ref.shape[0]
    taps = 2 * bases * (REACH + 1) // 2

    def part(c, j, row):
        start = c * taps + abs(j) * bases
        return proj[start : start + bases, row * cols : (row + 1) * cols]

    def smoothed(c, row):
        out = None
        for j in range(-REACH, REACH + 1):
            if 0 <= row + j < block_rows:
                term = part(c, j, row + j)
                out = term if out is None else out + term
        return out

    below = [block_rows, block_rows + 1]
    above = [-2, -1]
    slots = [(0, r) for r in range(block_rows)] + [(1, r) for r in range(block_rows)]
    slots += [(0, r) for r in below] + [(1, r) for r in below]
    slots += [(1, r) for r in above] + [(0, r) for r in above]
    for q, (c, row) in enumerate(slots):
        stage[q] = smoothed(c, row)
    flat = stage.reshape(len(slots) * bases, cols)
    own = bases // groups
    for d in range(groups):
        lines = [
            [
                flat[pl.ds(q * block_rows * bases + d * own + k, block_rows, stride=bases), :]
                for q in range(3)
            ]
            for k in range(own)
        ]
        rows = [v for k in range(own) for v in lines[k][:2]] + [lines[k][2] for k in range(own)]
        out_ref[d] = jnp.concatenate(rows, 0).astype(jnp.bfloat16)


def join_kernel(part_ref, low_ref, high_ref, out_ref):
    groups = part_ref.shape[0]
    own, _, rows, cols = out_ref.shape
    block_rows = rows // groups
    sub = lax.broadcasted_iota(jnp.int32, (block_rows, cols), 0)

    def lent(ref_value, k):
        start = k * block_rows
        return ref_value[start : start + block_rows].astype(jnp.float32)

    base = own * 2 * block_rows
    for k in range(own):
        lends = (
            [lent(low_ref[...], k)]
            + [lent(part_ref[b, base:, :], k) for b in range(groups)]
            + [lent(high_ref[...], k)]
        )
        for b in range(groups):
            for c in range(2):
                start = (k * 2 + c) * block_rows
                main = part_ref[b, start : start + block_rows, :].astype(jnp.float32)
                before = lends[b]
                after = lends[b + 2]
                if c == 1:
                    before = pltpu.roll(before, block_rows - 2, 0)
                    after = pltpu.roll(after, 2, 0)
                out_ref[k, c, b * block_rows : (b + 1) * block_rows, :] = (
                    main
                    + jnp.where(sub < 2, before, 0.0)
                    + jnp.where(sub >= block_rows - 2, after, 0.0)
                )


def on_chip(x):
    return pltpu.with_memory_space_constraint(x, pltpu.VMEM) if not INTERPRET else x


def chip_out(shape, dtype):
    return jax.ShapeDtypeStruct(shape, dtype) if INTERPRET else pltpu.VMEM(shape, dtype)


def vmem(count):
    return [pl.BlockSpec(memory_space=pltpu.VMEM)] * count


def shifts(axis):
    count = lax.axis_size(axis)
    forward = [(i, i + 1) for i in range(count - 1)]
    return forward, [(b, a) for a, b in forward]


def on_device(slc_stack, fir_taps, look_index, shrink_level, window_half, basis):
    date_local, rows, cols = slc_stack.shape[1:]
    groups = lax.axis_size("date")
    block_rows = rows // groups
    pixels = block_rows * cols
    bases, dates = basis.shape
    own = bases // groups
    forward, backward = shifts("az")

    edge_low = jnp.swapaxes(slc_stack[:, :, rows - REACH :, :], 1, 2)
    edge_high = jnp.swapaxes(slc_stack[:, :, :REACH, :], 1, 2)
    low = lax.ppermute(edge_low, "az", forward)
    high = lax.ppermute(edge_high, "az", backward)
    pitch = rows + 8
    blocks = pl.pallas_call(
        filter_kernel,
        out_shape=chip_out((groups, 2, date_local, pixels), jnp.bfloat16),
        in_specs=vmem(4),
        out_specs=vmem(1)[0],
        scratch_shapes=[pltpu.VMEM((date_local * pitch, cols), jnp.float32)],
        interpret=INTERPRET,
        name="azimuth_filter",
    )(slc_stack, on_chip(low), on_chip(high), fir_taps)
    pix = lax.all_to_all(blocks, "date", split_axis=0, concat_axis=0, tiled=True)

    look = look_index.reshape(1, -1)
    slots = 3 * block_rows
    height = 3 * own * block_rows
    lent = pl.pallas_call(
        link_kernel,
        out_shape=chip_out((groups, height, cols), jnp.bfloat16),
        in_specs=vmem(5),
        out_specs=vmem(1)[0],
        scratch_shapes=[pltpu.VMEM((slots, bases, cols), jnp.float32)],
        interpret=INTERPRET,
        name="phase_link",
    )(
        on_chip(pix),
        jnp.concatenate([look, look], 1),
        shrink_level,
        window_half.reshape(1, dates),
        basis,
    )
    parts = lax.all_to_all(lent, "date", split_axis=0, concat_axis=0, tiled=True)

    base = 2 * own * block_rows
    above = lax.ppermute(parts[0, base:, :], "az", backward)
    below = lax.ppermute(parts[groups - 1, base:, :], "az", forward)
    return pl.pallas_call(
        join_kernel,
        out_shape=jax.ShapeDtypeStruct((own, 2, rows, cols), jnp.float32),
        in_specs=vmem(3),
        out_specs=vmem(1)[0],
        interpret=INTERPRET,
        name="overlap_add",
    )(on_chip(parts), on_chip(below), on_chip(above))


def solution(mesh):
    in_specs = (
        P(None, "date", "az", None),
        P("date", None),
        P("az", "date", None),
        P("az", "date"),
        P(),
        P(),
    )
    out_specs = P("date", None, "az", None)
    return jax.shard_map(
        on_device, mesh=mesh, in_specs=in_specs, out_specs=out_specs, check_vma=False
    )
```

```python
import jax
import jax.numpy as jnp
from jax import lax
from jax.experimental import pallas as pl
from jax.experimental.pallas import tpu as pltpu
from jax.sharding import PartitionSpec as P

NS_ITERS = 6
REACH = 2
INTERPRET = False


def filter_kernel(
    odd_ref, slc_hbm, near_ref, far_ref, taps_ref, out_ref, slc_ref, held, done, load_sems, sems
):
    _, dates, rows, cols = slc_ref.shape
    blocks = out_ref.shape[0]
    block_rows = rows // blocks
    pitch = held.shape[0] // dates
    even = odd_ref[0, 0] == 0
    taps = [
        jnp.broadcast_to(taps_ref[:, j : j + 1], (dates, cols)) for j in range(2 * REACH + 1)
    ]
    parts = sems.shape[0] // 2
    share = blocks // parts
    copies = []
    loads = [
        pltpu.make_async_copy(slc_hbm.at[c], slc_ref.at[c], load_sems.at[c]) for c in range(2)
    ]
    for load in loads:
        load.start()
    for c in range(2):
        loads[c].wait()
        for t in range(dates):
            held[pl.ds(t * pitch, rows), :] = slc_ref[c, t].astype(jnp.float32)

        def line(r):
            if r < 0:
                pick = jnp.where(even, far_ref[c, r + REACH], near_ref[c, r + REACH])
                return pick.astype(jnp.float32)
            if r >= rows:
                pick = jnp.where(even, near_ref[c, r - rows], far_ref[c, r - rows])
                return pick.astype(jnp.float32)
            return held[pl.ds(r, dates, stride=pitch), :]

        window = [line(r) for r in range(-REACH, REACH)]
        for r in range(rows):
            window.append(line(r + REACH))
            total = taps[0] * window[0]
            for j in range(1, 2 * REACH + 1):
                total = total + taps[j] * window[j]
            window.pop(0)
            b, i = divmod(r, block_rows)
            done[b, c, :, i * cols : (i + 1) * cols] = total.astype(jnp.bfloat16)
            if (r + 1) % (share * block_rows) == 0:
                part = b // share
                copy = pltpu.make_async_copy(
                    done.at[pl.ds(part * share, share), c],
                    out_ref.at[pl.ds(part * share, share), c],
                    sems.at[c * parts + part],
                )
                copy.start()
                copies.append(copy)
    for copy in copies:
        copy.wait()


def split(x):
    hi = x.astype(jnp.bfloat16)
    return hi, (x - hi.astype(jnp.float32)).astype(jnp.bfloat16)


def dot(a, b):
    return jnp.dot(a, b, preferred_element_type=jnp.float32)


def dot3(a, b):
    a_hi, a_lo = split(a)
    b_hi, b_lo = split(b)
    return dot(
        jnp.concatenate([a_hi, a_lo, a_hi], 1), jnp.concatenate([b_hi, b_hi, b_lo], 0)
    )


def total(x):
    return jnp.sum(jnp.sum(x, axis=1, keepdims=True), axis=0, keepdims=True)


def link_kernel(
    date_ref, pix_ref, look_ref, level_ref, half_ref, basis_ref, stage_ref, edge_ref, proj
):
    groups, _, dates_own, pixels = pix_ref.shape
    dates = groups * dates_own
    width = look_ref.shape[1]
    looks = width // 2
    bases = basis_ref.shape[0]
    cols = stage_ref.shape[2]
    block_rows = pixels // cols
    place = lax.broadcasted_iota(jnp.int32, (pixels, width), 0)
    picked = (place == look_ref[...]).astype(jnp.float32).astype(jnp.bfloat16)
    samp_re = dot(pix_ref[:, 0].reshape(dates, pixels), picked)
    samp_im = dot(pix_ref[:, 1].reshape(dates, pixels), picked)
    first = lax.broadcasted_iota(jnp.int32, (dates, width), 1) < looks
    tall = jnp.concatenate(
        [jnp.where(first, samp_re, -samp_im), jnp.where(first, samp_im, samp_re)], 0
    )
    wide = tall.T.astype(jnp.bfloat16)
    tall = tall.astype(jnp.bfloat16)
    inner = dot(wide[:looks], tall)

    half = half_ref[...]
    share = basis_ref[...].astype(jnp.float32) / (2 * half + 1).astype(jnp.float32)
    near = jnp.concatenate(
        [jnp.where(half >= j, share, 0.0) for j in range(REACH + 1)], axis=0
    )
    near_hi, near_lo = split(near)
    seen = dot(near_hi, tall[:dates]) + dot(near_lo, tall[:dates])

    rows_i = lax.broadcasted_iota(jnp.int32, (looks, width), 0)
    cols_i = lax.broadcasted_iota(jnp.int32, (looks, width), 1)
    identity = (rows_i == cols_i).astype(jnp.float32)
    turn = jnp.where(cols_i < looks, -1.0, 1.0)

    def whole(top):
        return jnp.concatenate([top, turn * pltpu.roll(top, looks, 1)], 0)

    trace = total(inner * identity)
    square = total(inner * inner)
    mean = trace / (looks * dates) + 1e-06
    weight = level_ref[...].astype(jnp.float32) / 16.0
    alpha = weight * mean + mean
    beta = (1.0 - weight) / looks
    scale = 1.0 / jnp.sqrt(
        dates * alpha * alpha + 2.0 * alpha * beta * trace + beta * beta * square
    )

    t = scale * alpha
    x = jnp.ones_like(t)
    w = (scale * beta) * inner
    m = (2.0 - 2.0 * t) * identity - w
    u = -identity
    w = (2.0 - 2.0 * t) * w - dot3(w, whole(w))
    x, t = x * (2.0 - t), 2.0 * t - t * t
    for step in range(1, NS_ITERS):
        full = whole(w)
        if step < NS_ITERS - 1:
            w = (2.0 - 2.0 * t) * w - dot3(w, full)
        prod = dot3(jnp.concatenate([m, u], 0), full)
        m, u = (
            (2.0 - 2.0 * t) * m - prod[:looks],
            (2.0 - t) * u - x * m - prod[looks:],
        )
        x, t = x * (2.0 - t), 2.0 * t - t * t

    core = dot3(seen, whole((scale * beta) * (m - (mean * scale) * u)))
    core_hi, core_lo = split(core)
    gain = dot(core_hi, wide) + dot(core_lo, wide)
    plain = (t - mean * scale * x) * near
    left = gain[:, :dates] + plain
    right = gain[:, dates:]
    gain_re = jnp.concatenate([left, -right], 0).astype(jnp.bfloat16)
    gain_im = jnp.concatenate([right, left], 0).astype(jnp.bfloat16)
    proj[...] = dot(gain_re, pix_ref[:, 0].reshape(dates, pixels)) + dot(
        gain_im, pix_ref[:, 1].reshape(dates, pixels)
    )

    below = [block_rows, block_rows + 1]
    above = [-2, -1]
    slots = [(0, r) for r in range(block_rows)] + [(1, r) for r in range(block_rows)]
    slots += [(0, r) for r in below] + [(1, r) for r in below]
    slots += [(1, r) for r in above] + [(0, r) for r in above]
    sub = 8
    opens = date_ref[0, 0] == 0
    for k in range(0, bases, sub):
        rest = {}
        for c in range(2):
            terms = [
                [
                    proj[
                        pl.ds((c * (REACH + 1) + j) * bases + k, sub),
                        pl.ds(row * cols, cols),
                    ]
                    for row in range(block_rows)
                ]
                for j in range(REACH + 1)
            ]
            for q, (part, row) in enumerate(slots):
                if part != c:
                    continue
                out = None
                for j in range(-REACH, REACH + 1):
                    if 0 <= row + j < block_rows:
                        term = terms[abs(j)][row + j]
                        out = term if out is None else out + term
                stage_ref[q, pl.ds(k, sub), :] = out
                rest[q] = out
        base = 2 * block_rows
        for i in range(2 * REACH):
            edge = jnp.where(opens, rest[base + 2 * REACH + i], rest[base + i])
            edge_ref[i, pl.ds(k, sub), :] = edge.astype(jnp.bfloat16)


def pack_kernel(date_ref, stage_ref, edge_ref, out_ref, held):
    groups = out_ref.shape[0]
    slots, bases, cols = stage_ref.shape
    sub = slots // 3
    own = bases // groups
    opens = date_ref[0, 0] == 0
    closes = date_ref[0, 0] == groups - 1
    for q in range(slots):
        value = stage_ref[q]
        i = q - 2 * sub
        if i >= 2 * REACH:
            value = jnp.where(opens, edge_ref[i - 2 * REACH].astype(jnp.float32), value)
        elif i >= 0:
            value = jnp.where(closes, edge_ref[i].astype(jnp.float32), value)
        held[pl.ds(q * bases, bases), :] = value
    for d in range(groups):
        lines = [
            [
                held[pl.ds(q * sub * bases + d * own + k, sub, stride=bases), :]
                for q in range(3)
            ]
            for k in range(own)
        ]
        rows = [v for k in range(own) for v in lines[k][:2]] + [lines[k][2] for k in range(own)]
        out_ref[d] = jnp.concatenate(rows, 0).astype(jnp.bfloat16)


def join_kernel(part_ref, out_ref):
    groups = part_ref.shape[0]
    own, _, rows, cols = out_ref.shape
    block_rows = rows // groups
    sub = lax.broadcasted_iota(jnp.int32, (block_rows, cols), 0)
    base = own * 2 * block_rows
    for k in range(own):
        start = base + k * block_rows
        lends = [
            part_ref[b, start : start + block_rows, :].astype(jnp.float32)
            for b in range(groups)
        ]
        for b in range(groups):
            for c in range(2):
                start = (k * 2 + c) * block_rows
                main = part_ref[b, start : start + block_rows, :].astype(jnp.float32)
                if b:
                    before = pltpu.roll(lends[b - 1], block_rows - 2, 0) if c else lends[b - 1]
                else:
                    before = pltpu.roll(lends[0], 2 if c else 4, 0)
                if b < groups - 1:
                    after = pltpu.roll(lends[b + 1], 2, 0) if c else lends[b + 1]
                else:
                    after = pltpu.roll(lends[b], block_rows - 2 if c else 4, 0)
                out_ref[k, c, b * block_rows : (b + 1) * block_rows, :] = (
                    main
                    + jnp.where(sub < 2, before, 0.0)
                    + jnp.where(sub >= block_rows - 2, after, 0.0)
                )


def on_chip(x):
    return x if INTERPRET else pltpu.with_memory_space_constraint(x, pltpu.VMEM)


def chip_out(shape, dtype):
    return jax.ShapeDtypeStruct(shape, dtype) if INTERPRET else pltpu.VMEM(shape, dtype)


VMEM = pl.BlockSpec(memory_space=pltpu.VMEM)
ANY = pl.BlockSpec(memory_space=pl.ANY)
SMEM = pl.BlockSpec(memory_space=pltpu.SMEM)


def swaps(pairs):
    return [pair for a, b in pairs for pair in ((a, b), (b, a))]


def on_device(slc_stack, fir_taps, look_index, shrink_level, window_half, basis):
    date_local, rows, cols = slc_stack.shape[1:]
    groups = lax.axis_size("date")
    slabs = lax.axis_size("az")
    block_rows = rows // groups
    pixels = block_rows * cols
    bases, dates = basis.shape
    own = bases // groups

    odd = lax.axis_index("az") & 1
    last = jnp.swapaxes(slc_stack[:, :, rows - REACH :, :], 1, 2)
    start = jnp.swapaxes(slc_stack[:, :, :REACH, :], 1, 2)
    far = lax.ppermute(
        jnp.where(odd == 0, start, last),
        "az",
        swaps([(i, i + 1) for i in range(1, slabs - 1, 2)]),
    )
    near = lax.ppermute(
        jnp.where(odd == 0, last, start),
        "az",
        swaps([(i, i + 1) for i in range(0, slabs - 1, 2)]),
    )
    pitch = rows + 8
    shape = (groups, 2, date_local, pixels)
    blocks = pl.pallas_call(
        filter_kernel,
        out_shape=jax.ShapeDtypeStruct(shape, jnp.bfloat16),
        in_specs=[SMEM, ANY] + [VMEM] * 3,
        out_specs=ANY,
        scratch_shapes=[
            pltpu.VMEM(slc_stack.shape, jnp.bfloat16),
            pltpu.VMEM((date_local * pitch, cols), jnp.float32),
            pltpu.VMEM(shape, jnp.bfloat16),
            pltpu.SemaphoreType.DMA((2,)),
            pltpu.SemaphoreType.DMA((8,)),
        ],
        interpret=INTERPRET,
        name="azimuth_filter",
    )(odd.reshape(1, 1), slc_stack, on_chip(near), on_chip(far), fir_taps)
    pix = lax.all_to_all(blocks, "date", split_axis=0, concat_axis=0, tiled=True)

    date = lax.axis_index("date").reshape(1, 1)
    look = look_index.reshape(1, -1)
    slots = 3 * block_rows
    stage, edge = pl.pallas_call(
        link_kernel,
        out_shape=(
            chip_out((slots, bases, cols), jnp.float32),
            chip_out((2 * REACH, bases, cols), jnp.bfloat16),
        ),
        in_specs=[SMEM] + [VMEM] * 5,
        out_specs=(VMEM, VMEM),
        scratch_shapes=[pltpu.VMEM((2 * (REACH + 1) * bases, pixels), jnp.float32)],
        interpret=INTERPRET,
        name="phase_link",
    )(
        date,
        on_chip(pix),
        jnp.concatenate([look, look], 1),
        shrink_level,
        window_half.reshape(1, dates),
        basis,
    )
    edge = lax.ppermute(
        edge,
        ("date", "az"),
        swaps([((groups - 1) * slabs + a, a + 1) for a in range(slabs - 1)]),
    )
    lent = pl.pallas_call(
        pack_kernel,
        out_shape=chip_out((groups, 3 * own * block_rows, cols), jnp.bfloat16),
        in_specs=[SMEM, VMEM, VMEM],
        out_specs=VMEM,
        scratch_shapes=[pltpu.VMEM((slots * bases, cols), jnp.float32)],
        interpret=INTERPRET,
        name="pack_rows",
    )(date, on_chip(stage), on_chip(edge))
    parts = lax.all_to_all(lent, "date", split_axis=0, concat_axis=0, tiled=True)
    return pl.pallas_call(
        join_kernel,
        out_shape=jax.ShapeDtypeStruct((own, 2, rows, cols), jnp.float32),
        in_specs=[VMEM],
        out_specs=VMEM,
        interpret=INTERPRET,
        name="overlap_add",
    )(on_chip(parts))


def solution(mesh):
    in_specs = (
        P(None, "date", "az", None),
        P("date", None),
        P("az", "date", None),
        P("az", "date"),
        P(),
        P(),
    )
    out_specs = P("date", None, "az", None)
    return jax.shard_map(
        on_device, mesh=mesh, in_specs=in_specs, out_specs=out_specs, check_vma=False
    )
```

```python
import jax
import jax.numpy as jnp
from jax import lax
from jax.experimental import pallas as pl
from jax.experimental.pallas import tpu as pltpu
from jax.sharding import PartitionSpec as P

NS_ITERS = 6
REACH = 2
INTERPRET = False


def filter_kernel(
    slc_hbm,
    near_ref,
    far_ref,
    taps_ref,
    look_hbm,
    level_smem,
    half_hbm,
    basis_hbm,
    out_ref,
    look_ref,
    level_ref,
    half_ref,
    basis_ref,
    slc_ref,
    held,
    sems,
):
    _, dates, rows, cols = slc_ref.shape
    blocks = out_ref.shape[0]
    block_rows = rows // blocks
    pitch = held.shape[0] // dates
    even = (lax.axis_index("az") & 1) == 0
    columns = taps_ref[...].T
    taps = [
        jnp.broadcast_to(columns[:, j : j + 1], (dates, cols)) for j in range(2 * REACH + 1)
    ]
    loads = [
        pltpu.make_async_copy(slc_hbm.at[c], slc_ref.at[c], sems.at[c]) for c in range(2)
    ]
    small = [
        (look_hbm, look_ref),
        (half_hbm, half_ref),
        (basis_hbm, basis_ref),
    ]
    copies = [
        pltpu.make_async_copy(a, b, sems.at[2 + i]) for i, (a, b) in enumerate(small)
    ]
    for copy in loads + copies:
        copy.start()
    level_ref[...] = jnp.full(level_ref.shape, level_smem[0, 0].astype(jnp.float32))
    for c in range(2):
        loads[c].wait()
        for t in range(dates):
            held[pl.ds(t * pitch, rows), :] = slc_ref[c, t].astype(jnp.float32)

        def line(r):
            if r < 0:
                pick = jnp.where(even, far_ref[c, r + REACH], near_ref[c, r + REACH])
                return pick.astype(jnp.float32)
            if r >= rows:
                pick = jnp.where(even, near_ref[c, r - rows], far_ref[c, r - rows])
                return pick.astype(jnp.float32)
            return held[pl.ds(r, dates, stride=pitch), :]

        window = [line(r) for r in range(-REACH, REACH)]
        for r in range(rows):
            window.append(line(r + REACH))
            total = taps[0] * window[0]
            for j in range(1, 2 * REACH + 1):
                total = total + taps[j] * window[j]
            window.pop(0)
            b, i = divmod(r, block_rows)
            out_ref[b, c, :, i * cols : (i + 1) * cols] = total.astype(jnp.bfloat16)
    for copy in copies:
        copy.wait()


def split(x):
    hi = x.astype(jnp.bfloat16)
    return hi, (x - hi.astype(jnp.float32)).astype(jnp.bfloat16)


def dot(a, b):
    return jnp.dot(a, b, preferred_element_type=jnp.float32)


def dot3(a, b):
    a_hi, a_lo = split(a)
    b_hi, b_lo = split(b)
    return dot(
        jnp.concatenate([a_hi, a_lo, a_hi], 1), jnp.concatenate([b_hi, b_hi, b_lo], 0)
    )


def total(x):
    return jnp.sum(jnp.sum(x, axis=1, keepdims=True), axis=0, keepdims=True)


def link_kernel(
    pix_ref, look_ref, level_ref, half_ref, basis_ref, stage_ref, edge_ref, proj
):
    groups, _, dates_own, pixels = pix_ref.shape
    dates = groups * dates_own
    looks = look_ref.shape[1]
    width = 2 * looks
    bases = basis_ref.shape[0]
    cols = stage_ref.shape[2]
    block_rows = pixels // cols
    place = lax.broadcasted_iota(jnp.int32, (pixels, width), 0)
    chosen = jnp.concatenate([look_ref[...], look_ref[...]], 1)
    picked = (place == chosen).astype(jnp.float32).astype(jnp.bfloat16)
    samp_re = dot(pix_ref[:, 0].reshape(dates, pixels), picked)
    samp_im = dot(pix_ref[:, 1].reshape(dates, pixels), picked)
    first = lax.broadcasted_iota(jnp.int32, (dates, width), 1) < looks
    tall = jnp.concatenate(
        [jnp.where(first, samp_re, -samp_im), jnp.where(first, samp_im, samp_re)], 0
    )
    wide = tall.T.astype(jnp.bfloat16)
    tall = tall.astype(jnp.bfloat16)
    inner = dot(wide[:looks], tall)

    half = half_ref[...]
    share = basis_ref[...].astype(jnp.float32) / (2 * half + 1).astype(jnp.float32)
    near = jnp.concatenate(
        [jnp.where(half >= j, share, 0.0) for j in range(REACH + 1)], axis=0
    )
    near_hi, near_lo = split(near)
    seen = dot(near_hi, tall[:dates]) + dot(near_lo, tall[:dates])

    rows_i = lax.broadcasted_iota(jnp.int32, (looks, width), 0)
    cols_i = lax.broadcasted_iota(jnp.int32, (looks, width), 1)
    identity = (rows_i == cols_i).astype(jnp.float32)
    turn = jnp.where(cols_i < looks, -1.0, 1.0)

    def whole(top):
        return jnp.concatenate([top, turn * pltpu.roll(top, looks, 1)], 0)

    trace = total(inner * identity)
    square = total(inner * inner)
    mean = trace / (looks * dates) + 1e-06
    weight = level_ref[:, :1] / 16.0
    alpha = weight * mean + mean
    beta = (1.0 - weight) / looks
    scale = 1.0 / jnp.sqrt(
        dates * alpha * alpha + 2.0 * alpha * beta * trace + beta * beta * square
    )

    t = scale * alpha
    x = jnp.ones_like(t)
    w = (scale * beta) * inner
    m = (2.0 - 2.0 * t) * identity - w
    u = -identity
    w = (2.0 - 2.0 * t) * w - dot3(w, whole(w))
    x, t = x * (2.0 - t), 2.0 * t - t * t
    for step in range(1, NS_ITERS):
        full = whole(w)
        if step < NS_ITERS - 1:
            w = (2.0 - 2.0 * t) * w - dot3(w, full)
        prod = dot3(jnp.concatenate([m, u], 0), full)
        m, u = (
            (2.0 - 2.0 * t) * m - prod[:looks],
            (2.0 - t) * u - x * m - prod[looks:],
        )
        x, t = x * (2.0 - t), 2.0 * t - t * t

    core = dot3(seen, whole((scale * beta) * (m - (mean * scale) * u)))
    core_hi, core_lo = split(core)
    gain = dot(core_hi, wide) + dot(core_lo, wide)
    plain = (t - mean * scale * x) * near
    left = gain[:, :dates] + plain
    right = gain[:, dates:]
    gain_re = jnp.concatenate([left, -right], 0).astype(jnp.bfloat16)
    gain_im = jnp.concatenate([right, left], 0).astype(jnp.bfloat16)
    proj[...] = dot(gain_re, pix_ref[:, 0].reshape(dates, pixels)) + dot(
        gain_im, pix_ref[:, 1].reshape(dates, pixels)
    )

    below = [block_rows, block_rows + 1]
    above = [-2, -1]
    slots = [(0, r) for r in range(block_rows)] + [(1, r) for r in range(block_rows)]
    slots += [(0, r) for r in below] + [(1, r) for r in below]
    slots += [(1, r) for r in above] + [(0, r) for r in above]
    sub = 8
    opens = lax.axis_index("date") == 0
    for k in range(0, bases, sub):
        rest = {}
        for c in range(2):
            terms = [
                [
                    proj[
                        pl.ds((c * (REACH + 1) + j) * bases + k, sub),
                        pl.ds(row * cols, cols),
                    ]
                    for row in range(block_rows)
                ]
                for j in range(REACH + 1)
            ]
            for q, (part, row) in enumerate(slots):
                if part != c:
                    continue
                out = None
                for j in range(-REACH, REACH + 1):
                    if 0 <= row + j < block_rows:
                        term = terms[abs(j)][row + j]
                        out = term if out is None else out + term
                stage_ref[q, pl.ds(k, sub), :] = out
                rest[q] = out
        base = 2 * block_rows
        for i in range(2 * REACH):
            edge = jnp.where(opens, rest[base + 2 * REACH + i], rest[base + i])
            edge_ref[i, pl.ds(k, sub), :] = edge.astype(jnp.bfloat16)


def pack_kernel(stage_ref, edge_ref, out_ref, held):
    groups = out_ref.shape[0]
    slots, bases, cols = stage_ref.shape
    sub = slots // 3
    own = bases // groups
    opens = lax.axis_index("date") == 0
    closes = lax.axis_index("date") == groups - 1
    for q in range(slots):
        value = stage_ref[q]
        i = q - 2 * sub
        if i >= 2 * REACH:
            value = jnp.where(opens, edge_ref[i - 2 * REACH].astype(jnp.float32), value)
        elif i >= 0:
            value = jnp.where(closes, edge_ref[i].astype(jnp.float32), value)
        held[pl.ds(q * bases, bases), :] = value
    for d in range(groups):
        lines = [
            [
                held[pl.ds(q * sub * bases + d * own + k, sub, stride=bases), :]
                for q in range(3)
            ]
            for k in range(own)
        ]
        rows = [v for k in range(own) for v in lines[k][:2]] + [lines[k][2] for k in range(own)]
        out_ref[d] = jnp.concatenate(rows, 0).astype(jnp.bfloat16)


def join_kernel(part_ref, out_ref):
    groups = part_ref.shape[0]
    own, _, rows, cols = out_ref.shape
    block_rows = rows // groups
    sub = lax.broadcasted_iota(jnp.int32, (block_rows, cols), 0)
    base = own * 2 * block_rows
    for k in range(own):
        start = base + k * block_rows
        lends = [
            part_ref[b, start : start + block_rows, :].astype(jnp.float32)
            for b in range(groups)
        ]
        for b in range(groups):
            for c in range(2):
                start = (k * 2 + c) * block_rows
                main = part_ref[b, start : start + block_rows, :].astype(jnp.float32)
                before = lends[b - 1]
                after = lends[(b + 1) % groups]
                if c == 1:
                    before = pltpu.roll(before, block_rows - 2, 0)
                    after = pltpu.roll(after, 2, 0)
                out_ref[k, c, b * block_rows : (b + 1) * block_rows, :] = (
                    main
                    + jnp.where(sub < 2, before, 0.0)
                    + jnp.where(sub >= block_rows - 2, after, 0.0)
                )


def on_chip(x):
    return x if INTERPRET else pltpu.with_memory_space_constraint(x, pltpu.VMEM)


def chip_out(shape, dtype):
    return jax.ShapeDtypeStruct(shape, dtype) if INTERPRET else pltpu.VMEM(shape, dtype)


VMEM = pl.BlockSpec(memory_space=pltpu.VMEM)
ANY = pl.BlockSpec(memory_space=pl.ANY)
SMEM = pl.BlockSpec(memory_space=pltpu.SMEM)


def swaps(pairs):
    return [pair for a, b in pairs for pair in ((a, b), (b, a))]


def on_device(slc_stack, fir_taps, look_index, shrink_level, window_half, basis):
    date_local, rows, cols = slc_stack.shape[1:]
    groups = lax.axis_size("date")
    slabs = lax.axis_size("az")
    block_rows = rows // groups
    pixels = block_rows * cols
    bases, dates = basis.shape
    own = bases // groups

    odd = lax.axis_index("az") & 1
    last = jnp.swapaxes(slc_stack[:, :, rows - REACH :, :], 1, 2)
    start = jnp.swapaxes(slc_stack[:, :, :REACH, :], 1, 2)
    far = lax.ppermute(
        jnp.where(odd == 0, start, last),
        "az",
        swaps([(i, i + 1) for i in range(1, slabs - 1, 2)]),
    )
    near = lax.ppermute(
        jnp.where(odd == 0, last, start),
        "az",
        swaps([(i, i + 1) for i in range(0, slabs - 1, 2)]),
    )
    pitch = rows + 8
    shape = (groups, 2, date_local, pixels)
    look = look_index.reshape(1, -1)
    half = window_half.reshape(1, dates)
    blocks, look, level, half, basis = pl.pallas_call(
        filter_kernel,
        out_shape=(
            chip_out(shape, jnp.bfloat16),
            chip_out(look.shape, look.dtype),
            chip_out((1, cols), jnp.float32),
            chip_out(half.shape, half.dtype),
            chip_out(basis.shape, basis.dtype),
        ),
        in_specs=[ANY] + [VMEM] * 3 + [ANY, SMEM, ANY, ANY],
        out_specs=(VMEM,) * 5,
        scratch_shapes=[
            pltpu.VMEM(slc_stack.shape, jnp.bfloat16),
            pltpu.VMEM((date_local * pitch, cols), jnp.float32),
            pltpu.SemaphoreType.DMA((5,)),
        ],
        interpret=INTERPRET,
        name="azimuth_filter",
    )(
        slc_stack,
        on_chip(near),
        on_chip(far),
        on_chip(fir_taps.T),
        look,
        shrink_level,
        half,
        basis,
    )
    pix = lax.all_to_all(blocks, "date", split_axis=0, concat_axis=0, tiled=True)

    slots = 3 * block_rows
    stage, edge = pl.pallas_call(
        link_kernel,
        out_shape=(
            chip_out((slots, bases, cols), jnp.float32),
            chip_out((2 * REACH, bases, cols), jnp.bfloat16),
        ),
        in_specs=[VMEM] * 5,
        out_specs=(VMEM, VMEM),
        scratch_shapes=[pltpu.VMEM((2 * (REACH + 1) * bases, pixels), jnp.float32)],
        interpret=INTERPRET,
        name="phase_link",
    )(
        on_chip(pix),
        on_chip(look),
        on_chip(level),
        on_chip(half),
        on_chip(basis),
    )
    edge = lax.ppermute(
        edge,
        ("date", "az"),
        [((groups - 1) * slabs + a, (groups - 1) * slabs + a + 1) for a in range(slabs - 1)]
        + [(a + 1, a) for a in range(slabs - 1)],
    )
    lent = pl.pallas_call(
        pack_kernel,
        out_shape=chip_out((groups, 3 * own * block_rows, cols), jnp.bfloat16),
        in_specs=[VMEM, VMEM],
        out_specs=VMEM,
        scratch_shapes=[pltpu.VMEM((slots * bases, cols), jnp.float32)],
        interpret=INTERPRET,
        name="pack_rows",
    )(on_chip(stage), on_chip(edge))
    parts = lax.all_to_all(lent, "date", split_axis=0, concat_axis=0, tiled=True)
    return pl.pallas_call(
        join_kernel,
        out_shape=jax.ShapeDtypeStruct((own, 2, rows, cols), jnp.float32),
        in_specs=[VMEM],
        out_specs=VMEM,
        interpret=INTERPRET,
        name="overlap_add",
    )(on_chip(parts))


def solution(mesh):
    in_specs = (
        P(None, "date", "az", None),
        P("date", None),
        P("az", "date", None),
        P("az", "date"),
        P(),
        P(),
    )
    out_specs = P("date", None, "az", None)
    return jax.shard_map(
        on_device, mesh=mesh, in_specs=in_specs, out_specs=out_specs, check_vma=False
    )
```

```python
import jax
import jax.numpy as jnp
from jax import lax
from jax.experimental import pallas as pl
from jax.experimental.pallas import tpu as pltpu
from jax.sharding import PartitionSpec as P


NS_ITERS = 6
REACH = 2
INTERPRET = False


def spread(taps_ref, cols):
    columns = taps_ref[...].T
    return [
        jnp.broadcast_to(columns[:, j : j + 1], (columns.shape[0], cols))
        for j in range(2 * REACH + 1)
    ]


def weigh(taps, window):
    total = taps[0] * window[0]
    for j in range(1, 2 * REACH + 1):
        total = total + taps[j] * window[j]
    return total.astype(jnp.bfloat16)


def filter_kernel(
    slc_hbm,
    taps_ref,
    look_hbm,
    level_smem,
    half_hbm,
    basis_hbm,
    out_ref,
    rim_ref,
    look_ref,
    level_ref,
    half_ref,
    basis_ref,
    slc_ref,
    held,
    sems,
):
    _, dates, rows, cols = slc_ref.shape
    blocks = out_ref.shape[0]
    block_rows = rows // blocks
    pitch = held.shape[0] // dates
    taps = spread(taps_ref, cols)
    loads = [
        pltpu.make_async_copy(slc_hbm.at[c], slc_ref.at[c], sems.at[c]) for c in range(2)
    ]
    small = [
        (look_hbm, look_ref),
        (half_hbm, half_ref),
        (basis_hbm, basis_ref),
    ]
    copies = [
        pltpu.make_async_copy(a, b, sems.at[2 + i]) for i, (a, b) in enumerate(small)
    ]
    for copy in loads + copies:
        copy.start()
    level_ref[...] = jnp.full(level_ref.shape, level_smem[0, 0].astype(jnp.float32))
    for c in range(2):
        loads[c].wait()
        for t in range(dates):
            held[pl.ds(t * pitch, rows), :] = slc_ref[c, t].astype(jnp.float32)

        def line(r):
            return held[pl.ds(r, dates, stride=pitch), :]

        window = [line(r) for r in range(2 * REACH)]
        for i in range(2 * REACH):
            rim_ref[0, c, i] = window[i]
        for r in range(REACH, rows - REACH):
            window.append(line(r + REACH))
            b, i = divmod(r, block_rows)
            out_ref[b, c, :, i * cols : (i + 1) * cols] = weigh(taps, window)
            window.pop(0)
        for i in range(2 * REACH):
            rim_ref[1, c, i] = window[i]
    for copy in copies:
        copy.wait()


def rim_kernel(part_ref, rim_ref, near_ref, far_ref, taps_ref, out_ref):
    del part_ref
    blocks = out_ref.shape[0]
    cols = rim_ref.shape[-1]
    block_rows = out_ref.shape[-1] // cols
    even = (lax.axis_index("az") & 1) == 0
    taps = spread(taps_ref, cols)
    for c in range(2):
        own = [[rim_ref[side, c, i] for i in range(2 * REACH)] for side in range(2)]
        near = [near_ref[c, i].astype(jnp.float32) for i in range(REACH)]
        far = [far_ref[c, i].astype(jnp.float32) for i in range(REACH)]
        low = [jnp.where(even, b, a) for a, b in zip(near, far)] + own[0]
        high = own[1] + [jnp.where(even, a, b) for a, b in zip(near, far)]
        for i in range(REACH):
            window = slice(i, i + 2 * REACH + 1)
            out_ref[0, c, :, i * cols : (i + 1) * cols] = weigh(taps, low[window])
            row = block_rows - REACH + i
            out_ref[blocks - 1, c, :, row * cols : (row + 1) * cols] = weigh(
                taps, high[window]
            )


def split(x):
    hi = x.astype(jnp.bfloat16)
    return hi, (x - hi.astype(jnp.float32)).astype(jnp.bfloat16)


def dot(a, b):
    return jnp.dot(a, b, preferred_element_type=jnp.float32)


def dot3(a, b):
    a_hi, a_lo = split(a)
    b_hi, b_lo = split(b)
    return dot(
        jnp.concatenate([a_hi, a_lo, a_hi], 1), jnp.concatenate([b_hi, b_hi, b_lo], 0)
    )


def total(x):
    return jnp.sum(jnp.sum(x, axis=1, keepdims=True), axis=0, keepdims=True)


def link_kernel(
    pix_ref, look_ref, level_ref, half_ref, basis_ref, stage_ref, edge_ref, proj
):
    groups, _, dates_own, pixels = pix_ref.shape
    dates = groups * dates_own
    looks = look_ref.shape[1]
    width = 2 * looks
    bases = basis_ref.shape[0]
    cols = stage_ref.shape[2]
    block_rows = pixels // cols
    place = lax.broadcasted_iota(jnp.int32, (pixels, width), 0)
    chosen = jnp.concatenate([look_ref[...], look_ref[...]], 1)
    picked = (place == chosen).astype(jnp.float32).astype(jnp.bfloat16)
    samp_re = dot(pix_ref[:, 0].reshape(dates, pixels), picked)
    samp_im = dot(pix_ref[:, 1].reshape(dates, pixels), picked)
    first = lax.broadcasted_iota(jnp.int32, (dates, width), 1) < looks
    tall = jnp.concatenate(
        [jnp.where(first, samp_re, -samp_im), jnp.where(first, samp_im, samp_re)], 0
    )
    wide = tall.T.astype(jnp.bfloat16)
    tall = tall.astype(jnp.bfloat16)
    inner = dot(wide[:looks], tall)

    half = half_ref[...]
    share = basis_ref[...].astype(jnp.float32) / (2 * half + 1).astype(jnp.float32)
    near = jnp.concatenate(
        [jnp.where(half >= j, share, 0.0) for j in range(REACH + 1)], axis=0
    )
    near_hi, near_lo = split(near)
    seen = dot(near_hi, tall[:dates]) + dot(near_lo, tall[:dates])

    rows_i = lax.broadcasted_iota(jnp.int32, (looks, width), 0)
    cols_i = lax.broadcasted_iota(jnp.int32, (looks, width), 1)
    identity = (rows_i == cols_i).astype(jnp.float32)
    turn = jnp.where(cols_i < looks, -1.0, 1.0)

    def whole(top):
        return jnp.concatenate([top, turn * pltpu.roll(top, looks, 1)], 0)

    trace = total(inner * identity)
    square = total(inner * inner)
    mean = trace / (looks * dates) + 1e-06
    weight = level_ref[:, :1] / 16.0
    alpha = weight * mean + mean
    beta = (1.0 - weight) / looks
    scale = 1.0 / jnp.sqrt(
        dates * alpha * alpha + 2.0 * alpha * beta * trace + beta * beta * square
    )

    t = scale * alpha
    x = jnp.ones_like(t)
    w = (scale * beta) * inner
    m = (2.0 - 2.0 * t) * identity - w
    u = -identity
    w = (2.0 - 2.0 * t) * w - dot3(w, whole(w))
    x, t = x * (2.0 - t), 2.0 * t - t * t
    for step in range(1, NS_ITERS):
        full = whole(w)
        if step < NS_ITERS - 1:
            w = (2.0 - 2.0 * t) * w - dot3(w, full)
        prod = dot3(jnp.concatenate([m, u], 0), full)
        m, u = (
            (2.0 - 2.0 * t) * m - prod[:looks],
            (2.0 - t) * u - x * m - prod[looks:],
        )
        x, t = x * (2.0 - t), 2.0 * t - t * t

    core = dot3(seen, whole((scale * beta) * (m - (mean * scale) * u)))
    core_hi, core_lo = split(core)
    gain = dot(core_hi, wide) + dot(core_lo, wide)
    plain = (t - mean * scale * x) * near
    left = gain[:, :dates] + plain
    right = gain[:, dates:]
    gain_re = jnp.concatenate([left, -right], 0).astype(jnp.bfloat16)
    gain_im = jnp.concatenate([right, left], 0).astype(jnp.bfloat16)
    proj[...] = dot(gain_re, pix_ref[:, 0].reshape(dates, pixels)) + dot(
        gain_im, pix_ref[:, 1].reshape(dates, pixels)
    )

    below = [block_rows, block_rows + 1]
    above = [-2, -1]
    slots = [(0, r) for r in range(block_rows)] + [(1, r) for r in range(block_rows)]
    slots += [(0, r) for r in below] + [(1, r) for r in below]
    slots += [(1, r) for r in above] + [(0, r) for r in above]
    sub = 8
    opens = lax.axis_index("date") == 0
    for k in range(0, bases, sub):
        rest = {}
        for c in range(2):
            terms = [
                [
                    proj[
                        pl.ds((c * (REACH + 1) + j) * bases + k, sub),
                        pl.ds(row * cols, cols),
                    ]
                    for row in range(block_rows)
                ]
                for j in range(REACH + 1)
            ]
            for q, (part, row) in enumerate(slots):
                if part != c:
                    continue
                out = None
                for j in range(-REACH, REACH + 1):
                    if 0 <= row + j < block_rows:
                        term = terms[abs(j)][row + j]
                        out = term if out is None else out + term
                stage_ref[q, pl.ds(k, sub), :] = out
                rest[q] = out
        base = 2 * block_rows
        for i in range(2 * REACH):
            edge = jnp.where(opens, rest[base + 2 * REACH + i], rest[base + i])
            edge_ref[i, pl.ds(k, sub), :] = edge.astype(jnp.bfloat16)


def pack_kernel(stage_ref, edge_ref, out_ref, held):
    groups = out_ref.shape[0]
    slots, bases, _ = stage_ref.shape
    sub = slots // 3
    own = bases // groups
    opens = lax.axis_index("date") == 0
    closes = lax.axis_index("date") == groups - 1
    for q in range(slots):
        value = stage_ref[q]
        i = q - 2 * sub
        if i >= 2 * REACH:
            value = jnp.where(opens, edge_ref[i - 2 * REACH].astype(jnp.float32), value)
        elif i >= 0:
            value = jnp.where(closes, edge_ref[i].astype(jnp.float32), value)
        held[pl.ds(q * bases, bases), :] = value
    for d in range(groups):
        lines = [
            [
                held[pl.ds(q * sub * bases + d * own + k, sub, stride=bases), :]
                for q in range(3)
            ]
            for k in range(own)
        ]
        rows = [v for k in range(own) for v in lines[k][:2]] + [lines[k][2] for k in range(own)]
        out_ref[d] = jnp.concatenate(rows, 0).astype(jnp.bfloat16)


def join_kernel(part_ref, out_ref):
    groups = part_ref.shape[0]
    own, _, rows, cols = out_ref.shape
    block_rows = rows // groups
    sub = lax.broadcasted_iota(jnp.int32, (block_rows, cols), 0)
    base = own * 2 * block_rows
    for k in range(own):
        start = base + k * block_rows
        lends = [
            part_ref[b, start : start + block_rows, :].astype(jnp.float32)
            for b in range(groups)
        ]
        for b in range(groups):
            for c in range(2):
                start = (k * 2 + c) * block_rows
                main = part_ref[b, start : start + block_rows, :].astype(jnp.float32)
                before = lends[b - 1]
                after = lends[(b + 1) % groups]
                if c == 1:
                    before = pltpu.roll(before, block_rows - 2, 0)
                    after = pltpu.roll(after, 2, 0)
                out_ref[k, c, b * block_rows : (b + 1) * block_rows, :] = (
                    main
                    + jnp.where(sub < 2, before, 0.0)
                    + jnp.where(sub >= block_rows - 2, after, 0.0)
                )


def on_chip(x):
    return x if INTERPRET else pltpu.with_memory_space_constraint(x, pltpu.VMEM)


def chip_out(shape, dtype):
    return jax.ShapeDtypeStruct(shape, dtype) if INTERPRET else pltpu.VMEM(shape, dtype)


VMEM = pl.BlockSpec(memory_space=pltpu.VMEM)
ANY = pl.BlockSpec(memory_space=pl.ANY)
SMEM = pl.BlockSpec(memory_space=pltpu.SMEM)


def swaps(pairs):
    return [pair for a, b in pairs for pair in ((a, b), (b, a))]


def on_device(slc_stack, fir_taps, look_index, shrink_level, window_half, basis):
    date_local, rows, cols = slc_stack.shape[1:]
    groups = lax.axis_size("date")
    slabs = lax.axis_size("az")
    block_rows = rows // groups
    pixels = block_rows * cols
    bases, dates = basis.shape
    own = bases // groups

    odd = lax.axis_index("az") & 1
    last = jnp.swapaxes(slc_stack[:, :, rows - REACH :, :], 1, 2)
    start = jnp.swapaxes(slc_stack[:, :, :REACH, :], 1, 2)
    far = lax.ppermute(
        jnp.where(odd == 0, start, last),
        "az",
        swaps([(i, i + 1) for i in range(1, slabs - 1, 2)]),
    )
    near = lax.ppermute(
        jnp.where(odd == 0, last, start),
        "az",
        swaps([(i, i + 1) for i in range(0, slabs - 1, 2)]),
    )
    pitch = rows + 8
    shape = (groups, 2, date_local, pixels)
    look = look_index.reshape(1, -1)
    half = window_half.reshape(1, dates)
    taps = fir_taps.T
    blocks, rim, look, level, half, basis = pl.pallas_call(
        filter_kernel,
        out_shape=(
            chip_out(shape, jnp.bfloat16),
            chip_out((2, 2, 2 * REACH, date_local, cols), jnp.float32),
            chip_out(look.shape, look.dtype),
            chip_out((1, cols), jnp.float32),
            chip_out(half.shape, half.dtype),
            chip_out(basis.shape, basis.dtype),
        ),
        in_specs=[ANY, VMEM, ANY, SMEM, ANY, ANY],
        out_specs=(VMEM,) * 6,
        scratch_shapes=[
            pltpu.VMEM(slc_stack.shape, jnp.bfloat16),
            pltpu.VMEM((date_local * pitch, cols), jnp.float32),
            pltpu.SemaphoreType.DMA((5,)),
        ],
        interpret=INTERPRET,
        name="azimuth_filter",
    )(slc_stack, on_chip(taps), look, shrink_level, half, basis)
    blocks = pl.pallas_call(
        rim_kernel,
        out_shape=chip_out(shape, jnp.bfloat16),
        in_specs=[VMEM] * 5,
        out_specs=VMEM,
        input_output_aliases={0: 0},
        interpret=INTERPRET,
        name="filter_rim",
    )(on_chip(blocks), on_chip(rim), on_chip(near), on_chip(far), on_chip(taps))
    pix = lax.all_to_all(blocks, "date", split_axis=0, concat_axis=0, tiled=True)

    slots = 3 * block_rows
    stage, edge = pl.pallas_call(
        link_kernel,
        out_shape=(
            chip_out((slots, bases, cols), jnp.float32),
            chip_out((2 * REACH, bases, cols), jnp.bfloat16),
        ),
        in_specs=[VMEM] * 5,
        out_specs=(VMEM, VMEM),
        scratch_shapes=[pltpu.VMEM((2 * (REACH + 1) * bases, pixels), jnp.float32)],
        interpret=INTERPRET,
        name="phase_link",
    )(
        on_chip(pix),
        on_chip(look),
        on_chip(level),
        on_chip(half),
        on_chip(basis),
    )
    edge = lax.ppermute(
        edge,
        ("date", "az"),
        [((groups - 1) * slabs + a, (groups - 1) * slabs + a + 1) for a in range(slabs - 1)]
        + [(a + 1, a) for a in range(slabs - 1)],
    )
    lent = pl.pallas_call(
        pack_kernel,
        out_shape=chip_out((groups, 3 * own * block_rows, cols), jnp.bfloat16),
        in_specs=[VMEM, VMEM],
        out_specs=VMEM,
        scratch_shapes=[pltpu.VMEM((slots * bases, cols), jnp.float32)],
        interpret=INTERPRET,
        name="pack_rows",
    )(on_chip(stage), on_chip(edge))
    parts = lax.all_to_all(lent, "date", split_axis=0, concat_axis=0, tiled=True)
    return pl.pallas_call(
        join_kernel,
        out_shape=jax.ShapeDtypeStruct((own, 2, rows, cols), jnp.float32),
        in_specs=[VMEM],
        out_specs=VMEM,
        interpret=INTERPRET,
        name="overlap_add",
    )(on_chip(parts))


def solution(mesh):
    in_specs = (
        P(None, "date", "az", None),
        P("date", None),
        P("az", "date", None),
        P("az", "date"),
        P(),
        P(),
    )
    out_specs = P("date", None, "az", None)
    return jax.shard_map(
        on_device, mesh=mesh, in_specs=in_specs, out_specs=out_specs, check_vma=False
    )
```

```python
import jax
import jax.numpy as jnp
from jax import lax
from jax.experimental import pallas as pl
from jax.experimental.pallas import tpu as pltpu
from jax.sharding import PartitionSpec as P


NS_ITERS = 6
REACH = 2
INTERPRET = False


def spread(taps_ref, cols):
    columns = taps_ref[...].T
    return [
        jnp.broadcast_to(columns[:, j : j + 1], (columns.shape[0], cols))
        for j in range(2 * REACH + 1)
    ]


def weigh(taps, window):
    total = taps[0] * window[0]
    for j in range(1, 2 * REACH + 1):
        total = total + taps[j] * window[j]
    return total.astype(jnp.bfloat16)


def filter_kernel(
    slc_hbm,
    taps_ref,
    look_hbm,
    level_smem,
    half_hbm,
    basis_hbm,
    out_ref,
    rim_ref,
    look_ref,
    level_ref,
    half_ref,
    basis_ref,
    slc_ref,
    held,
    sems,
):
    _, dates, rows, cols = slc_ref.shape
    blocks = out_ref.shape[0]
    block_rows = rows // blocks
    pitch = held.shape[0] // dates
    taps = spread(taps_ref, cols)
    loads = [
        pltpu.make_async_copy(slc_hbm.at[c], slc_ref.at[c], sems.at[c]) for c in range(2)
    ]
    small = [
        (look_hbm, look_ref),
        (half_hbm, half_ref),
        (basis_hbm, basis_ref),
    ]
    copies = [
        pltpu.make_async_copy(a, b, sems.at[2 + i]) for i, (a, b) in enumerate(small)
    ]
    for copy in loads + copies:
        copy.start()
    level_ref[...] = jnp.full(level_ref.shape, level_smem[0, 0].astype(jnp.float32))
    for c in range(2):
        loads[c].wait()
        for t in range(dates):
            held[pl.ds(t * pitch, rows), :] = slc_ref[c, t].astype(jnp.float32)

        def line(r):
            return held[pl.ds(r, dates, stride=pitch), :]

        window = [line(r) for r in range(2 * REACH)]
        for i in range(2 * REACH):
            rim_ref[0, c, i] = window[i]
        for r in range(REACH, rows - REACH):
            window.append(line(r + REACH))
            b, i = divmod(r, block_rows)
            out_ref[b, c, :, i * cols : (i + 1) * cols] = weigh(taps, window)
            window.pop(0)
        for i in range(2 * REACH):
            rim_ref[1, c, i] = window[i]
    for copy in copies:
        copy.wait()


def rim_kernel(part_ref, rim_ref, near_ref, far_ref, taps_ref, out_ref):
    del part_ref
    blocks = out_ref.shape[0]
    cols = rim_ref.shape[-1]
    block_rows = out_ref.shape[-1] // cols
    even = (lax.axis_index("az") & 1) == 0
    taps = spread(taps_ref, cols)
    for c in range(2):
        own = [[rim_ref[side, c, i] for i in range(2 * REACH)] for side in range(2)]
        near = [near_ref[c, i].astype(jnp.float32) for i in range(REACH)]
        far = [far_ref[c, i].astype(jnp.float32) for i in range(REACH)]
        low = [jnp.where(even, b, a) for a, b in zip(near, far)] + own[0]
        high = own[1] + [jnp.where(even, a, b) for a, b in zip(near, far)]
        for i in range(REACH):
            window = slice(i, i + 2 * REACH + 1)
            out_ref[0, c, :, i * cols : (i + 1) * cols] = weigh(taps, low[window])
            row = block_rows - REACH + i
            out_ref[blocks - 1, c, :, row * cols : (row + 1) * cols] = weigh(
                taps, high[window]
            )


def split(x):
    hi = x.astype(jnp.bfloat16)
    return hi, (x - hi.astype(jnp.float32)).astype(jnp.bfloat16)


def dot(a, b):
    return jnp.dot(a, b, preferred_element_type=jnp.float32)


def dot3(a, b):
    a_hi, a_lo = split(a)
    b_hi, b_lo = split(b)
    return dot(
        jnp.concatenate([a_hi, a_lo, a_hi], 1), jnp.concatenate([b_hi, b_hi, b_lo], 0)
    )


def total(x):
    return jnp.sum(jnp.sum(x, axis=1, keepdims=True), axis=0, keepdims=True)


def link_kernel(
    pix_ref, look_ref, level_ref, half_ref, basis_ref, gain_ref, edge_ref
):
    groups, _, dates_own, pixels = pix_ref.shape
    dates = groups * dates_own
    looks = look_ref.shape[1]
    width = 2 * looks
    bases = basis_ref.shape[0]
    cols = edge_ref.shape[2]
    place = lax.broadcasted_iota(jnp.int32, (pixels, width), 0)
    chosen = jnp.concatenate([look_ref[...], look_ref[...]], 1)
    picked = (place == chosen).astype(jnp.float32).astype(jnp.bfloat16)
    samp_re = dot(pix_ref[:, 0].reshape(dates, pixels), picked)
    samp_im = dot(pix_ref[:, 1].reshape(dates, pixels), picked)
    first = lax.broadcasted_iota(jnp.int32, (dates, width), 1) < looks
    tall = jnp.concatenate(
        [jnp.where(first, samp_re, -samp_im), jnp.where(first, samp_im, samp_re)], 0
    )
    wide = tall.T.astype(jnp.bfloat16)
    tall = tall.astype(jnp.bfloat16)
    inner = dot(wide[:looks], tall)

    half = half_ref[...]
    share = basis_ref[...].astype(jnp.float32) / (2 * half + 1).astype(jnp.float32)
    near = jnp.concatenate(
        [jnp.where(half >= j, share, 0.0) for j in range(REACH + 1)], axis=0
    )
    near_hi, near_lo = split(near)
    seen = dot(near_hi, tall[:dates]) + dot(near_lo, tall[:dates])

    rows_i = lax.broadcasted_iota(jnp.int32, (looks, width), 0)
    cols_i = lax.broadcasted_iota(jnp.int32, (looks, width), 1)
    identity = (rows_i == cols_i).astype(jnp.float32)
    turn = jnp.where(cols_i < looks, -1.0, 1.0)

    def whole(top):
        return jnp.concatenate([top, turn * pltpu.roll(top, looks, 1)], 0)

    trace = total(inner * identity)
    square = total(inner * inner)
    mean = trace / (looks * dates) + 1e-06
    weight = level_ref[:, :1] / 16.0
    alpha = weight * mean + mean
    beta = (1.0 - weight) / looks
    scale = 1.0 / jnp.sqrt(
        dates * alpha * alpha + 2.0 * alpha * beta * trace + beta * beta * square
    )

    t = scale * alpha
    x = jnp.ones_like(t)
    w = (scale * beta) * inner
    m = (2.0 - 2.0 * t) * identity - w
    u = -identity
    w = (2.0 - 2.0 * t) * w - dot3(w, whole(w))
    x, t = x * (2.0 - t), 2.0 * t - t * t
    for step in range(1, NS_ITERS):
        full = whole(w)
        if step < NS_ITERS - 1:
            w = (2.0 - 2.0 * t) * w - dot3(w, full)
        prod = dot3(jnp.concatenate([m, u], 0), full)
        m, u = (
            (2.0 - 2.0 * t) * m - prod[:looks],
            (2.0 - t) * u - x * m - prod[looks:],
        )
        x, t = x * (2.0 - t), 2.0 * t - t * t

    core = dot3(seen, whole((scale * beta) * (m - (mean * scale) * u)))
    core_hi, core_lo = split(core)
    gain = dot(core_hi, wide) + dot(core_lo, wide)
    plain = (t - mean * scale * x) * near
    left = gain[:, :dates] + plain
    right = gain[:, dates:]
    gain_re = jnp.concatenate([left, -right], 0).astype(jnp.bfloat16)
    gain_im = jnp.concatenate([right, left], 0).astype(jnp.bfloat16)
    gain_ref[:, :dates] = gain_re
    gain_ref[:, dates:] = gain_im

    opens = lax.axis_index("date") == 0
    side = pl.multiple_of(jnp.where(opens, 0, pixels - REACH * cols), cols)
    outer = [
        pix_ref[:, c, :, pl.ds(side, REACH * cols)].reshape(dates, REACH * cols)
        for c in range(2)
    ]
    rows = (REACH + 1) * bases
    tops, bottoms = {}, {}
    for c in range(2):
        lines = slice(c * rows + bases, (c + 1) * rows)
        proj = dot(gain_re[lines], outer[0]) + dot(gain_im[lines], outer[1])

        def part(j, row):
            return proj[(j - 1) * bases : j * bases, row * cols : (row + 1) * cols]

        above = [part(2, 0), part(1, 0) + part(2, 1)]
        below = [part(2, 0) + part(1, 1), part(2, 1)]
        tops[c] = above
        bottoms[c] = below
    up = tops[1] + tops[0]
    down = bottoms[0] + bottoms[1]
    for i in range(2 * REACH):
        edge_ref[i] = jnp.where(opens, up[i], down[i]).astype(jnp.bfloat16)


def project_kernel(pix_ref, gain_ref, out_ref, lent_ref, proj, stage):
    groups, _, dates_own, pixels = pix_ref.shape
    dates = groups * dates_own
    bases, cols = lent_ref.shape[1:]
    block_rows = pixels // cols
    proj[...] = dot(gain_ref[:, :dates], pix_ref[:, 0].reshape(dates, pixels)) + dot(
        gain_ref[:, dates:], pix_ref[:, 1].reshape(dates, pixels)
    )
    below = [block_rows, block_rows + 1]
    above = [-2, -1]
    slots = [(0, r) for r in range(block_rows)] + [(1, r) for r in range(block_rows)]
    slots += [(0, r) for r in below] + [(1, r) for r in below]
    slots += [(1, r) for r in above] + [(0, r) for r in above]
    inner = 2 * block_rows
    sub = 8
    for k in range(0, bases, sub):
        for c in range(2):
            terms = [
                [
                    proj[
                        pl.ds((c * (REACH + 1) + j) * bases + k, sub),
                        pl.ds(row * cols, cols),
                    ]
                    for row in range(block_rows)
                ]
                for j in range(REACH + 1)
            ]
            for q, (part, row) in enumerate(slots):
                if part != c:
                    continue
                out = None
                for j in range(-REACH, REACH + 1):
                    if 0 <= row + j < block_rows:
                        term = terms[abs(j)][row + j]
                        out = term if out is None else out + term
                if q < inner:
                    stage[pl.ds(q * bases + k, sub), :] = out
                else:
                    lent_ref[q - inner, pl.ds(k, sub), :] = out
    own = bases // groups
    for d in range(groups):
        rows = [
            stage[pl.ds(c * block_rows * bases + d * own + k, block_rows, stride=bases), :]
            for k in range(own)
            for c in range(2)
        ]
        out_ref[d, : len(rows) * block_rows, :] = jnp.concatenate(rows, 0).astype(
            jnp.bfloat16
        )


def pack_kernel(part_ref, lent_ref, edge_ref, out_ref, held):
    del part_ref
    groups, height, _ = out_ref.shape
    slots, bases, _ = lent_ref.shape
    own = bases // groups
    opens = lax.axis_index("date") == 0
    closes = lax.axis_index("date") == groups - 1
    for i in range(slots):
        value = lent_ref[i]
        if i >= 2 * REACH:
            value = jnp.where(opens, edge_ref[i - 2 * REACH].astype(jnp.float32), value)
        else:
            value = jnp.where(closes, edge_ref[i].astype(jnp.float32), value)
        held[pl.ds(i * bases, bases), :] = value
    for d in range(groups):
        rows = [held[pl.ds(d * own + k, slots, stride=bases), :] for k in range(own)]
        out_ref[d, height - own * slots :, :] = jnp.concatenate(rows, 0).astype(jnp.bfloat16)


def join_kernel(part_ref, out_ref):
    groups = part_ref.shape[0]
    own, _, rows, cols = out_ref.shape
    block_rows = rows // groups
    sub = lax.broadcasted_iota(jnp.int32, (block_rows, cols), 0)
    base = own * 2 * block_rows
    for k in range(own):
        start = base + k * block_rows
        lends = [
            part_ref[b, start : start + block_rows, :].astype(jnp.float32)
            for b in range(groups)
        ]
        for b in range(groups):
            for c in range(2):
                start = (k * 2 + c) * block_rows
                main = part_ref[b, start : start + block_rows, :].astype(jnp.float32)
                before = lends[b - 1]
                after = lends[(b + 1) % groups]
                if c == 1:
                    before = pltpu.roll(before, block_rows - 2, 0)
                    after = pltpu.roll(after, 2, 0)
                out_ref[k, c, b * block_rows : (b + 1) * block_rows, :] = (
                    main
                    + jnp.where(sub < 2, before, 0.0)
                    + jnp.where(sub >= block_rows - 2, after, 0.0)
                )


def on_chip(x):
    return x if INTERPRET else pltpu.with_memory_space_constraint(x, pltpu.VMEM)


def chip_out(shape, dtype):
    return jax.ShapeDtypeStruct(shape, dtype) if INTERPRET else pltpu.VMEM(shape, dtype)


VMEM = pl.BlockSpec(memory_space=pltpu.VMEM)
ANY = pl.BlockSpec(memory_space=pl.ANY)
SMEM = pl.BlockSpec(memory_space=pltpu.SMEM)


def swaps(pairs):
    return [pair for a, b in pairs for pair in ((a, b), (b, a))]


def on_device(slc_stack, fir_taps, look_index, shrink_level, window_half, basis):
    date_local, rows, cols = slc_stack.shape[1:]
    groups = lax.axis_size("date")
    slabs = lax.axis_size("az")
    block_rows = rows // groups
    pixels = block_rows * cols
    bases, dates = basis.shape
    own = bases // groups

    odd = lax.axis_index("az") & 1
    last = jnp.swapaxes(slc_stack[:, :, rows - REACH :, :], 1, 2)
    start = jnp.swapaxes(slc_stack[:, :, :REACH, :], 1, 2)
    far = lax.ppermute(
        jnp.where(odd == 0, start, last),
        "az",
        swaps([(i, i + 1) for i in range(1, slabs - 1, 2)]),
    )
    near = lax.ppermute(
        jnp.where(odd == 0, last, start),
        "az",
        swaps([(i, i + 1) for i in range(0, slabs - 1, 2)]),
    )
    pitch = rows + 8
    shape = (groups, 2, date_local, pixels)
    look = look_index.reshape(1, -1)
    half = window_half.reshape(1, dates)
    taps = fir_taps.T
    blocks, rim, look, level, half, basis = pl.pallas_call(
        filter_kernel,
        out_shape=(
            chip_out(shape, jnp.bfloat16),
            chip_out((2, 2, 2 * REACH, date_local, cols), jnp.float32),
            chip_out(look.shape, look.dtype),
            chip_out((1, cols), jnp.float32),
            chip_out(half.shape, half.dtype),
            chip_out(basis.shape, basis.dtype),
        ),
        in_specs=[ANY, VMEM, ANY, SMEM, ANY, ANY],
        out_specs=(VMEM,) * 6,
        scratch_shapes=[
            pltpu.VMEM(slc_stack.shape, jnp.bfloat16),
            pltpu.VMEM((date_local * pitch, cols), jnp.float32),
            pltpu.SemaphoreType.DMA((5,)),
        ],
        interpret=INTERPRET,
        name="azimuth_filter",
    )(slc_stack, on_chip(taps), look, shrink_level, half, basis)
    blocks = pl.pallas_call(
        rim_kernel,
        out_shape=chip_out(shape, jnp.bfloat16),
        in_specs=[VMEM] * 5,
        out_specs=VMEM,
        input_output_aliases={0: 0},
        interpret=INTERPRET,
        name="filter_rim",
    )(on_chip(blocks), on_chip(rim), on_chip(near), on_chip(far), on_chip(taps))
    pix = lax.all_to_all(blocks, "date", split_axis=0, concat_axis=0, tiled=True)

    pix = on_chip(pix)
    rows_all = 2 * (REACH + 1) * bases
    gain, edge = pl.pallas_call(
        link_kernel,
        out_shape=(
            chip_out((rows_all, 2 * dates), jnp.bfloat16),
            chip_out((2 * REACH, bases, cols), jnp.bfloat16),
        ),
        in_specs=[VMEM] * 5,
        out_specs=(VMEM, VMEM),
        interpret=INTERPRET,
        name="phase_link",
    )(pix, on_chip(look), on_chip(level), on_chip(half), on_chip(basis))
    edge = lax.ppermute(
        edge,
        ("date", "az"),
        [((groups - 1) * slabs + a, (groups - 1) * slabs + a + 1) for a in range(slabs - 1)]
        + [(a + 1, a) for a in range(slabs - 1)],
    )
    packed = (groups, 3 * own * block_rows, cols)
    own_rows, lent = pl.pallas_call(
        project_kernel,
        out_shape=(
            chip_out(packed, jnp.bfloat16),
            chip_out((4 * REACH, bases, cols), jnp.float32),
        ),
        in_specs=[VMEM, VMEM],
        out_specs=(VMEM, VMEM),
        scratch_shapes=[
            pltpu.VMEM((rows_all, pixels), jnp.float32),
            pltpu.VMEM((2 * block_rows * bases, cols), jnp.float32),
        ],
        interpret=INTERPRET,
        name="project",
    )(pix, on_chip(gain))
    lent = pl.pallas_call(
        pack_kernel,
        out_shape=chip_out(packed, jnp.bfloat16),
        in_specs=[VMEM] * 3,
        out_specs=VMEM,
        scratch_shapes=[pltpu.VMEM((4 * REACH * bases, cols), jnp.float32)],
        input_output_aliases={0: 0},
        interpret=INTERPRET,
        name="pack_rows",
    )(on_chip(own_rows), on_chip(lent), on_chip(edge))
    parts = lax.all_to_all(lent, "date", split_axis=0, concat_axis=0, tiled=True)
    return pl.pallas_call(
        join_kernel,
        out_shape=jax.ShapeDtypeStruct((own, 2, rows, cols), jnp.float32),
        in_specs=[VMEM],
        out_specs=VMEM,
        interpret=INTERPRET,
        name="overlap_add",
    )(on_chip(parts))


def solution(mesh):
    in_specs = (
        P(None, "date", "az", None),
        P("date", None),
        P("az", "date", None),
        P("az", "date"),
        P(),
        P(),
    )
    out_specs = P("date", None, "az", None)
    return jax.shard_map(
        on_device, mesh=mesh, in_specs=in_specs, out_specs=out_specs, check_vma=False
    )
```

```python
import jax
import jax.numpy as jnp
from jax import lax
from jax.experimental import pallas as pl
from jax.experimental.pallas import tpu as pltpu
from jax.sharding import PartitionSpec as P


NS_ITERS = 6
REACH = 2
INTERPRET = False


def spread(taps_ref, cols):
    columns = taps_ref[...].T
    return [
        jnp.broadcast_to(columns[:, j : j + 1], (columns.shape[0], cols))
        for j in range(2 * REACH + 1)
    ]


def weigh(taps, window):
    total = taps[0] * window[0]
    for j in range(1, 2 * REACH + 1):
        total = total + taps[j] * window[j]
    return total.astype(jnp.bfloat16)


def fetch_kernel(
    slc_hbm,
    taps_hbm,
    look_hbm,
    half_hbm,
    basis_hbm,
    slc_ref,
    near_ref,
    far_ref,
    taps_ref,
    look_ref,
    half_ref,
    basis_ref,
    held,
    sems,
):
    _, dates, rows, _ = slc_ref.shape
    tile = held.shape[0] // dates
    spans = [(0, tile), (rows - tile, tile), (tile, rows - 2 * tile)]
    loads = [
        pltpu.make_async_copy(
            slc_hbm.at[:, :, pl.ds(start, size), :],
            slc_ref.at[:, :, pl.ds(start, size), :],
            sems.at[i],
        )
        for i, (start, size) in enumerate(spans)
    ]
    small = [
        (taps_hbm, taps_ref),
        (look_hbm, look_ref),
        (half_hbm, half_ref),
        (basis_hbm, basis_ref),
    ]
    loads += [
        pltpu.make_async_copy(a, b, sems.at[len(spans) + i])
        for i, (a, b) in enumerate(small)
    ]
    for load in loads:
        load.start()
    even = (lax.axis_index("az") & 1) == 0
    loads[0].wait()
    loads[1].wait()
    for c in range(2):
        edges = []
        for start, row in ((0, 0), (rows - tile, tile - REACH)):
            for t in range(dates):
                held[pl.ds(t * tile, tile), :] = slc_ref[
                    c, t, pl.ds(start, tile), :
                ].astype(jnp.float32)
            edges.append(
                [held[pl.ds(row + i, dates, stride=tile), :] for i in range(REACH)]
            )
        for i in range(REACH):
            first, last = edges[0][i], edges[1][i]
            near_ref[c, i] = jnp.where(even, last, first).astype(jnp.bfloat16)
            far_ref[c, i] = jnp.where(even, first, last).astype(jnp.bfloat16)
    for load in loads[2:]:
        load.wait()


def filter_kernel(slc_ref, taps_ref, level_smem, out_ref, rim_ref, level_ref, held):
    _, dates, rows, cols = slc_ref.shape
    blocks = out_ref.shape[0]
    block_rows = rows // blocks
    pitch = held.shape[0] // dates
    taps = spread(taps_ref, cols)
    level_ref[...] = jnp.full(level_ref.shape, level_smem[0, 0].astype(jnp.float32))
    for c in range(2):
        for t in range(dates):
            held[pl.ds(t * pitch, rows), :] = slc_ref[c, t].astype(jnp.float32)

        def line(r):
            return held[pl.ds(r, dates, stride=pitch), :]

        window = [line(r) for r in range(2 * REACH)]
        for i in range(2 * REACH):
            rim_ref[0, c, i] = window[i]
        for r in range(REACH, rows - REACH):
            window.append(line(r + REACH))
            b, i = divmod(r, block_rows)
            out_ref[b, c, :, i * cols : (i + 1) * cols] = weigh(taps, window)
            window.pop(0)
        for i in range(2 * REACH):
            rim_ref[1, c, i] = window[i]


def rim_kernel(part_ref, rim_ref, near_ref, far_ref, taps_ref, out_ref):
    del part_ref
    blocks = out_ref.shape[0]
    cols = rim_ref.shape[-1]
    block_rows = out_ref.shape[-1] // cols
    even = (lax.axis_index("az") & 1) == 0
    taps = spread(taps_ref, cols)
    for c in range(2):
        own = [[rim_ref[side, c, i] for i in range(2 * REACH)] for side in range(2)]
        near = [near_ref[c, i].astype(jnp.float32) for i in range(REACH)]
        far = [far_ref[c, i].astype(jnp.float32) for i in range(REACH)]
        low = [jnp.where(even, b, a) for a, b in zip(near, far)] + own[0]
        high = own[1] + [jnp.where(even, a, b) for a, b in zip(near, far)]
        for i in range(REACH):
            window = slice(i, i + 2 * REACH + 1)
            out_ref[0, c, :, i * cols : (i + 1) * cols] = weigh(taps, low[window])
            row = block_rows - REACH + i
            out_ref[blocks - 1, c, :, row * cols : (row + 1) * cols] = weigh(
                taps, high[window]
            )


def split(x):
    hi = x.astype(jnp.bfloat16)
    return hi, (x - hi.astype(jnp.float32)).astype(jnp.bfloat16)


def dot(a, b):
    return jnp.dot(a, b, preferred_element_type=jnp.float32)


def dot3(a, b):
    a_hi, a_lo = split(a)
    b_hi, b_lo = split(b)
    return dot(
        jnp.concatenate([a_hi, a_lo, a_hi], 1), jnp.concatenate([b_hi, b_hi, b_lo], 0)
    )


def total(x):
    return jnp.sum(jnp.sum(x, axis=1, keepdims=True), axis=0, keepdims=True)


def link_kernel(
    pix_ref, look_ref, level_ref, half_ref, basis_ref, gain_ref, edge_ref
):
    groups, _, dates_own, pixels = pix_ref.shape
    dates = groups * dates_own
    looks = look_ref.shape[1]
    width = 2 * looks
    bases = basis_ref.shape[0]
    cols = edge_ref.shape[2]
    place = lax.broadcasted_iota(jnp.int32, (pixels, width), 0)
    chosen = jnp.concatenate([look_ref[...], look_ref[...]], 1)
    picked = (place == chosen).astype(jnp.float32).astype(jnp.bfloat16)
    samp_re = dot(pix_ref[:, 0].reshape(dates, pixels), picked)
    samp_im = dot(pix_ref[:, 1].reshape(dates, pixels), picked)
    first = lax.broadcasted_iota(jnp.int32, (dates, width), 1) < looks
    tall = jnp.concatenate(
        [jnp.where(first, samp_re, -samp_im), jnp.where(first, samp_im, samp_re)], 0
    )
    wide = tall.T.astype(jnp.bfloat16)
    tall = tall.astype(jnp.bfloat16)
    inner = dot(wide[:looks], tall)

    half = half_ref[...]
    share = basis_ref[...].astype(jnp.float32) / (2 * half + 1).astype(jnp.float32)
    near = jnp.concatenate(
        [jnp.where(half >= j, share, 0.0) for j in range(REACH + 1)], axis=0
    )
    near_hi, near_lo = split(near)
    seen = dot(near_hi, tall[:dates]) + dot(near_lo, tall[:dates])

    rows_i = lax.broadcasted_iota(jnp.int32, (looks, width), 0)
    cols_i = lax.broadcasted_iota(jnp.int32, (looks, width), 1)
    identity = (rows_i == cols_i).astype(jnp.float32)
    turn = jnp.where(cols_i < looks, -1.0, 1.0)

    def whole(top):
        return jnp.concatenate([top, turn * pltpu.roll(top, looks, 1)], 0)

    trace = total(inner * identity)
    square = total(inner * inner)
    mean = trace / (looks * dates) + 1e-06
    weight = level_ref[:, :1] / 16.0
    alpha = weight * mean + mean
    beta = (1.0 - weight) / looks
    scale = 1.0 / jnp.sqrt(
        dates * alpha * alpha + 2.0 * alpha * beta * trace + beta * beta * square
    )

    t = scale * alpha
    x = jnp.ones_like(t)
    w = (scale * beta) * inner
    full = whole(w)
    m = (2.0 - 2.0 * t) * seen - dot3(seen, full)
    u = -seen
    w = (2.0 - 2.0 * t) * w - dot3(w, full)
    x, t = x * (2.0 - t), 2.0 * t - t * t
    for step in range(1, NS_ITERS):
        full = whole(w)
        if step < NS_ITERS - 1:
            w = (2.0 - 2.0 * t) * w - dot3(w, full)
        prod = dot3(jnp.concatenate([m, u], 0), full)
        m, u = (
            (2.0 - 2.0 * t) * m - prod[: m.shape[0]],
            (2.0 - t) * u - x * m - prod[m.shape[0] :],
        )
        x, t = x * (2.0 - t), 2.0 * t - t * t

    core = (scale * beta) * (m - (mean * scale) * u)
    core_hi, core_lo = split(core)
    gain = dot(core_hi, wide) + dot(core_lo, wide)
    plain = (t - mean * scale * x) * near
    left = gain[:, :dates] + plain
    right = gain[:, dates:]
    gain_re = jnp.concatenate([left, -right], 0).astype(jnp.bfloat16)
    gain_im = jnp.concatenate([right, left], 0).astype(jnp.bfloat16)
    gain_ref[:, :dates] = gain_re
    gain_ref[:, dates:] = gain_im

    opens = lax.axis_index("date") == 0
    side = pl.multiple_of(jnp.where(opens, 0, pixels - REACH * cols), cols)
    outer = [
        pix_ref[:, c, :, pl.ds(side, REACH * cols)].reshape(dates, REACH * cols)
        for c in range(2)
    ]
    rows = (REACH + 1) * bases
    tops, bottoms = {}, {}
    for c in range(2):
        lines = slice(c * rows + bases, (c + 1) * rows)
        proj = dot(gain_re[lines], outer[0]) + dot(gain_im[lines], outer[1])

        def part(j, row):
            return proj[(j - 1) * bases : j * bases, row * cols : (row + 1) * cols]

        above = [part(2, 0), part(1, 0) + part(2, 1)]
        below = [part(2, 0) + part(1, 1), part(2, 1)]
        tops[c] = above
        bottoms[c] = below
    up = tops[1] + tops[0]
    down = bottoms[0] + bottoms[1]
    for i in range(2 * REACH):
        edge_ref[i] = jnp.where(opens, up[i], down[i]).astype(jnp.bfloat16)


def project_kernel(pix_ref, gain_ref, out_ref, lent_ref, proj, stage):
    groups, _, dates_own, pixels = pix_ref.shape
    dates = groups * dates_own
    bases, cols = lent_ref.shape[1:]
    block_rows = pixels // cols
    proj[...] = dot(gain_ref[:, :dates], pix_ref[:, 0].reshape(dates, pixels)) + dot(
        gain_ref[:, dates:], pix_ref[:, 1].reshape(dates, pixels)
    )
    below = [block_rows, block_rows + 1]
    above = [-2, -1]
    slots = [(0, r) for r in range(block_rows)] + [(1, r) for r in range(block_rows)]
    slots += [(0, r) for r in below] + [(1, r) for r in below]
    slots += [(1, r) for r in above] + [(0, r) for r in above]
    inner = 2 * block_rows
    sub = 8
    for k in range(0, bases, sub):
        for c in range(2):
            terms = [
                [
                    proj[
                        pl.ds((c * (REACH + 1) + j) * bases + k, sub),
                        pl.ds(row * cols, cols),
                    ]
                    for row in range(block_rows)
                ]
                for j in range(REACH + 1)
            ]
            for q, (part, row) in enumerate(slots):
                if part != c:
                    continue
                out = None
                for j in range(-REACH, REACH + 1):
                    if 0 <= row + j < block_rows:
                        term = terms[abs(j)][row + j]
                        out = term if out is None else out + term
                if q < inner:
                    stage[pl.ds(q * bases + k, sub), :] = out
                else:
                    lent_ref[q - inner, pl.ds(k, sub), :] = out
    own = bases // groups
    for d in range(groups):
        rows = [
            stage[pl.ds(c * block_rows * bases + d * own + k, block_rows, stride=bases), :]
            for k in range(own)
            for c in range(2)
        ]
        out_ref[d, : len(rows) * block_rows, :] = jnp.concatenate(rows, 0).astype(
            jnp.bfloat16
        )


def pack_kernel(part_ref, lent_ref, edge_ref, out_ref, held):
    del part_ref
    groups, height, _ = out_ref.shape
    slots, bases, _ = lent_ref.shape
    own = bases // groups
    opens = lax.axis_index("date") == 0
    closes = lax.axis_index("date") == groups - 1
    for i in range(slots):
        value = lent_ref[i]
        if i >= 2 * REACH:
            value = jnp.where(opens, edge_ref[i - 2 * REACH].astype(jnp.float32), value)
        else:
            value = jnp.where(closes, edge_ref[i].astype(jnp.float32), value)
        held[pl.ds(i * bases, bases), :] = value
    for d in range(groups):
        rows = [held[pl.ds(d * own + k, slots, stride=bases), :] for k in range(own)]
        out_ref[d, height - own * slots :, :] = jnp.concatenate(rows, 0).astype(jnp.bfloat16)


def join_kernel(part_ref, out_ref):
    groups = part_ref.shape[0]
    own, _, rows, cols = out_ref.shape
    block_rows = rows // groups
    sub = lax.broadcasted_iota(jnp.int32, (block_rows, cols), 0)
    base = own * 2 * block_rows
    for k in range(own):
        start = base + k * block_rows
        lends = [
            part_ref[b, start : start + block_rows, :].astype(jnp.float32)
            for b in range(groups)
        ]
        for b in range(groups):
            for c in range(2):
                start = (k * 2 + c) * block_rows
                main = part_ref[b, start : start + block_rows, :].astype(jnp.float32)
                before = lends[b - 1]
                after = lends[(b + 1) % groups]
                if c == 1:
                    before = pltpu.roll(before, block_rows - 2, 0)
                    after = pltpu.roll(after, 2, 0)
                out_ref[k, c, b * block_rows : (b + 1) * block_rows, :] = (
                    main
                    + jnp.where(sub < 2, before, 0.0)
                    + jnp.where(sub >= block_rows - 2, after, 0.0)
                )


def on_chip(x):
    return x if INTERPRET else pltpu.with_memory_space_constraint(x, pltpu.VMEM)


def chip_out(shape, dtype):
    return jax.ShapeDtypeStruct(shape, dtype) if INTERPRET else pltpu.VMEM(shape, dtype)


VMEM = pl.BlockSpec(memory_space=pltpu.VMEM)
ANY = pl.BlockSpec(memory_space=pl.ANY)
SMEM = pl.BlockSpec(memory_space=pltpu.SMEM)


def swaps(pairs):
    return [pair for a, b in pairs for pair in ((a, b), (b, a))]


def on_device(slc_stack, fir_taps, look_index, shrink_level, window_half, basis):
    date_local, rows, cols = slc_stack.shape[1:]
    groups = lax.axis_size("date")
    slabs = lax.axis_size("az")
    block_rows = rows // groups
    pixels = block_rows * cols
    bases, dates = basis.shape
    own = bases // groups

    rim_shape = (2, REACH, date_local, cols)
    small = (fir_taps.T, look_index.reshape(1, -1), window_half.reshape(1, dates), basis)
    fetched, near, far, taps, look, half, basis = pl.pallas_call(
        fetch_kernel,
        out_shape=(
            chip_out(slc_stack.shape, jnp.bfloat16),
            chip_out(rim_shape, jnp.bfloat16),
            chip_out(rim_shape, jnp.bfloat16),
        )
        + tuple(chip_out(x.shape, x.dtype) for x in small),
        in_specs=[ANY] * 5,
        out_specs=(VMEM,) * 7,
        scratch_shapes=[
            pltpu.VMEM((date_local * 16, cols), jnp.float32),
            pltpu.SemaphoreType.DMA((7,)),
        ],
        interpret=INTERPRET,
        name="fetch",
    )(slc_stack, *small)
    near = lax.ppermute(near, "az", swaps([(i, i + 1) for i in range(0, slabs - 1, 2)]))
    far = lax.ppermute(far, "az", swaps([(i, i + 1) for i in range(1, slabs - 1, 2)]))
    pitch = rows + 8
    shape = (groups, 2, date_local, pixels)
    blocks, rim, level = pl.pallas_call(
        filter_kernel,
        out_shape=(
            chip_out(shape, jnp.bfloat16),
            chip_out((2, 2, 2 * REACH, date_local, cols), jnp.float32),
            chip_out((1, cols), jnp.float32),
        ),
        in_specs=[VMEM, VMEM, SMEM],
        out_specs=(VMEM,) * 3,
        scratch_shapes=[pltpu.VMEM((date_local * pitch, cols), jnp.float32)],
        interpret=INTERPRET,
        name="azimuth_filter",
    )(on_chip(fetched), on_chip(taps), shrink_level)
    blocks = pl.pallas_call(
        rim_kernel,
        out_shape=chip_out(shape, jnp.bfloat16),
        in_specs=[VMEM] * 5,
        out_specs=VMEM,
        input_output_aliases={0: 0},
        interpret=INTERPRET,
        name="filter_rim",
    )(on_chip(blocks), on_chip(rim), on_chip(near), on_chip(far), on_chip(taps))
    pix = lax.all_to_all(blocks, "date", split_axis=0, concat_axis=0, tiled=True)

    pix = on_chip(pix)
    rows_all = 2 * (REACH + 1) * bases
    gain, edge = pl.pallas_call(
        link_kernel,
        out_shape=(
            chip_out((rows_all, 2 * dates), jnp.bfloat16),
            chip_out((2 * REACH, bases, cols), jnp.bfloat16),
        ),
        in_specs=[VMEM] * 5,
        out_specs=(VMEM, VMEM),
        interpret=INTERPRET,
        name="phase_link",
    )(pix, on_chip(look), on_chip(level), on_chip(half), on_chip(basis))
    edge = lax.ppermute(
        edge,
        ("date", "az"),
        [((groups - 1) * slabs + a, (groups - 1) * slabs + a + 1) for a in range(slabs - 1)]
        + [(a + 1, a) for a in range(slabs - 1)],
    )
    packed = (groups, 3 * own * block_rows, cols)
    own_rows, lent = pl.pallas_call(
        project_kernel,
        out_shape=(
            chip_out(packed, jnp.bfloat16),
            chip_out((4 * REACH, bases, cols), jnp.float32),
        ),
        in_specs=[VMEM, VMEM],
        out_specs=(VMEM, VMEM),
        scratch_shapes=[
            pltpu.VMEM((rows_all, pixels), jnp.float32),
            pltpu.VMEM((2 * block_rows * bases, cols), jnp.float32),
        ],
        interpret=INTERPRET,
        name="project",
    )(pix, on_chip(gain))
    lent = pl.pallas_call(
        pack_kernel,
        out_shape=chip_out(packed, jnp.bfloat16),
        in_specs=[VMEM] * 3,
        out_specs=VMEM,
        scratch_shapes=[pltpu.VMEM((4 * REACH * bases, cols), jnp.float32)],
        input_output_aliases={0: 0},
        interpret=INTERPRET,
        name="pack_rows",
    )(on_chip(own_rows), on_chip(lent), on_chip(edge))
    parts = lax.all_to_all(lent, "date", split_axis=0, concat_axis=0, tiled=True)
    return pl.pallas_call(
        join_kernel,
        out_shape=jax.ShapeDtypeStruct((own, 2, rows, cols), jnp.float32),
        in_specs=[VMEM],
        out_specs=VMEM,
        interpret=INTERPRET,
        name="overlap_add",
    )(on_chip(parts))


def solution(mesh):
    in_specs = (
        P(None, "date", "az", None),
        P("date", None),
        P("az", "date", None),
        P("az", "date"),
        P(),
        P(),
    )
    out_specs = P("date", None, "az", None)
    return jax.shard_map(
        on_device, mesh=mesh, in_specs=in_specs, out_specs=out_specs, check_vma=False
    )
```

```python
import jax
import jax.numpy as jnp
from jax import lax
from jax.experimental import pallas as pl
from jax.experimental.pallas import tpu as pltpu
from jax.sharding import PartitionSpec as P


NS_ITERS = 6
REACH = 2
INTERPRET = False


def spread(taps_ref, cols):
    columns = taps_ref[...].T
    return [
        jnp.broadcast_to(columns[:, j : j + 1], (columns.shape[0], cols))
        for j in range(2 * REACH + 1)
    ]


def weigh(taps, window):
    total = taps[0] * window[0]
    for j in range(1, 2 * REACH + 1):
        total = total + taps[j] * window[j]
    return total.astype(jnp.bfloat16)


def fetch_kernel(
    slc_hbm,
    taps_hbm,
    look_hbm,
    half_hbm,
    basis_hbm,
    slc_ref,
    near_ref,
    far_ref,
    taps_ref,
    look_ref,
    half_ref,
    basis_ref,
    held,
    sems,
):
    _, dates, rows, _ = slc_ref.shape
    tile = held.shape[0] // dates
    parts = 4
    share = dates // parts
    spans = [(pl.ds(0, 2), pl.ds(0, dates), 0, tile)]
    spans += [(pl.ds(0, 2), pl.ds(0, dates), rows - tile, tile)]
    spans += [
        (pl.ds(c, 1), pl.ds(i * share, share), tile, rows - 2 * tile)
        for c in range(2)
        for i in range(parts)
    ]
    loads = [
        pltpu.make_async_copy(
            slc_hbm.at[c, t, pl.ds(start, size), :],
            slc_ref.at[c, t, pl.ds(start, size), :],
            sems.at[i],
        )
        for i, (c, t, start, size) in enumerate(spans)
    ]
    small = [
        (taps_hbm, taps_ref),
        (look_hbm, look_ref),
        (half_hbm, half_ref),
        (basis_hbm, basis_ref),
    ]
    loads += [
        pltpu.make_async_copy(a, b, sems.at[len(spans) + i])
        for i, (a, b) in enumerate(small)
    ]
    for load in loads:
        load.start()
    even = (lax.axis_index("az") & 1) == 0
    loads[0].wait()
    loads[1].wait()
    for c in range(2):
        edges = []
        for start, row in ((0, 0), (rows - tile, tile - REACH)):
            for t in range(dates):
                held[pl.ds(t * tile, tile), :] = slc_ref[
                    c, t, pl.ds(start, tile), :
                ].astype(jnp.float32)
            edges.append(
                [held[pl.ds(row + i, dates, stride=tile), :] for i in range(REACH)]
            )
        for i in range(REACH):
            first, last = edges[0][i], edges[1][i]
            near_ref[c, i] = jnp.where(even, last, first).astype(jnp.bfloat16)
            far_ref[c, i] = jnp.where(even, first, last).astype(jnp.bfloat16)
    for load in loads[2:]:
        load.wait()


def filter_kernel(slc_ref, taps_ref, level_smem, out_ref, rim_ref, level_ref, held):
    _, dates, rows, cols = slc_ref.shape
    blocks = out_ref.shape[0]
    block_rows = rows // blocks
    pitch = held.shape[0] // dates
    taps = spread(taps_ref, cols)
    level_ref[...] = jnp.full(level_ref.shape, level_smem[0, 0].astype(jnp.float32))
    for c in range(2):
        for t in range(dates):
            held[pl.ds(t * pitch, rows), :] = slc_ref[c, t].astype(jnp.float32)

        def line(r):
            return held[pl.ds(r, dates, stride=pitch), :]

        window = [line(r) for r in range(2 * REACH)]
        for i in range(2 * REACH):
            rim_ref[0, c, i] = window[i]
        for r in range(REACH, rows - REACH):
            window.append(line(r + REACH))
            b, i = divmod(r, block_rows)
            out_ref[b, c, :, i * cols : (i + 1) * cols] = weigh(taps, window)
            window.pop(0)
        for i in range(2 * REACH):
            rim_ref[1, c, i] = window[i]


def rim_kernel(part_ref, rim_ref, near_ref, far_ref, taps_ref, out_ref):
    del part_ref
    blocks = out_ref.shape[0]
    cols = rim_ref.shape[-1]
    block_rows = out_ref.shape[-1] // cols
    even = (lax.axis_index("az") & 1) == 0
    taps = spread(taps_ref, cols)
    for c in range(2):
        own = [[rim_ref[side, c, i] for i in range(2 * REACH)] for side in range(2)]
        near = [near_ref[c, i].astype(jnp.float32) for i in range(REACH)]
        far = [far_ref[c, i].astype(jnp.float32) for i in range(REACH)]
        low = [jnp.where(even, b, a) for a, b in zip(near, far)] + own[0]
        high = own[1] + [jnp.where(even, a, b) for a, b in zip(near, far)]
        for i in range(REACH):
            window = slice(i, i + 2 * REACH + 1)
            out_ref[0, c, :, i * cols : (i + 1) * cols] = weigh(taps, low[window])
            row = block_rows - REACH + i
            out_ref[blocks - 1, c, :, row * cols : (row + 1) * cols] = weigh(
                taps, high[window]
            )


def split(x):
    hi = x.astype(jnp.bfloat16)
    return hi, (x - hi.astype(jnp.float32)).astype(jnp.bfloat16)


def dot(a, b):
    return jnp.dot(a, b, preferred_element_type=jnp.float32)


def dot3(a, b):
    a_hi, a_lo = split(a)
    b_hi, b_lo = split(b)
    return dot(
        jnp.concatenate([a_hi, a_lo, a_hi], 1), jnp.concatenate([b_hi, b_hi, b_lo], 0)
    )


def total(x):
    return jnp.sum(jnp.sum(x, axis=1, keepdims=True), axis=0, keepdims=True)


def link_kernel(
    pix_ref, look_ref, level_ref, half_ref, basis_ref, gain_ref, edge_ref
):
    groups, _, dates_own, pixels = pix_ref.shape
    dates = groups * dates_own
    looks = look_ref.shape[1]
    width = 2 * looks
    bases = basis_ref.shape[0]
    cols = edge_ref.shape[2]
    place = lax.broadcasted_iota(jnp.int32, (pixels, width), 0)
    chosen = jnp.concatenate([look_ref[...], look_ref[...]], 1)
    picked = (place == chosen).astype(jnp.float32).astype(jnp.bfloat16)
    samp_re = dot(pix_ref[:, 0].reshape(dates, pixels), picked)
    samp_im = dot(pix_ref[:, 1].reshape(dates, pixels), picked)
    first = lax.broadcasted_iota(jnp.int32, (dates, width), 1) < looks
    tall = jnp.concatenate(
        [jnp.where(first, samp_re, -samp_im), jnp.where(first, samp_im, samp_re)], 0
    )
    tall = tall.astype(jnp.bfloat16)
    wide = tall.T
    inner = dot(wide[:looks], tall)

    half = half_ref[...]
    share = basis_ref[...].astype(jnp.float32) / (2 * half + 1).astype(jnp.float32)
    near = jnp.concatenate(
        [jnp.where(half >= j, share, 0.0) for j in range(REACH + 1)], axis=0
    )
    seen = dot(
        jnp.concatenate(split(near), 1), jnp.concatenate([tall[:dates], tall[:dates]], 0)
    )

    cols_i = lax.broadcasted_iota(jnp.int32, (looks, width), 1)
    turn = jnp.where(cols_i < looks, -1.0, 1.0)

    def whole(top):
        return jnp.concatenate([top, turn * pltpu.roll(top, looks, 1)], 0)

    trace = total(samp_re * samp_re + samp_im * samp_im) * 0.5
    square = total(inner * inner)
    mean = trace / (looks * dates) + 1e-06
    weight = level_ref[:, :1] / 16.0
    alpha = weight * mean + mean
    beta = (1.0 - weight) / looks
    scale = 1.0 / jnp.sqrt(
        dates * alpha * alpha + 2.0 * alpha * beta * trace + beta * beta * square
    )

    t = scale * alpha
    x = jnp.ones_like(t)
    w = (scale * beta) * inner
    full = whole(w)
    m = (2.0 - 2.0 * t) * seen - dot3(seen, full)
    u = -seen
    w = (2.0 - 2.0 * t) * w - dot3(w, full)
    x, t = x * (2.0 - t), 2.0 * t - t * t
    for step in range(1, NS_ITERS):
        full = whole(w)
        if step < NS_ITERS - 1:
            w = (2.0 - 2.0 * t) * w - dot3(w, full)
        prod = dot3(jnp.concatenate([m, u], 0), full)
        m, u = (
            (2.0 - 2.0 * t) * m - prod[: m.shape[0]],
            (2.0 - t) * u - x * m - prod[m.shape[0] :],
        )
        x, t = x * (2.0 - t), 2.0 * t - t * t

    core = (scale * beta) * (m - (mean * scale) * u)
    gain = dot(jnp.concatenate(split(core), 1), jnp.concatenate([wide, wide], 0))
    plain = (t - mean * scale * x) * near
    left = gain[:, :dates] + plain
    right = gain[:, dates:]
    gain_re = jnp.concatenate([left, -right], 0).astype(jnp.bfloat16)
    gain_im = jnp.concatenate([right, left], 0).astype(jnp.bfloat16)
    gain_ref[:, :dates] = gain_re
    gain_ref[:, dates:] = gain_im

    opens = lax.axis_index("date") == 0
    side = pl.multiple_of(jnp.where(opens, 0, pixels - REACH * cols), cols)
    outer = [
        pix_ref[:, c, :, pl.ds(side, REACH * cols)].reshape(dates, REACH * cols)
        for c in range(2)
    ]
    rows = (REACH + 1) * bases
    tops, bottoms = {}, {}
    for c in range(2):
        lines = slice(c * rows + bases, (c + 1) * rows)
        proj = dot(gain_re[lines], outer[0]) + dot(gain_im[lines], outer[1])

        def part(j, row):
            return proj[(j - 1) * bases : j * bases, row * cols : (row + 1) * cols]

        above = [part(2, 0), part(1, 0) + part(2, 1)]
        below = [part(2, 0) + part(1, 1), part(2, 1)]
        tops[c] = above
        bottoms[c] = below
    up = tops[1] + tops[0]
    down = bottoms[0] + bottoms[1]
    for i in range(2 * REACH):
        edge_ref[i] = jnp.where(opens, up[i], down[i]).astype(jnp.bfloat16)


def project_kernel(pix_ref, gain_ref, out_ref, lent_ref, proj, stage):
    groups, _, dates_own, pixels = pix_ref.shape
    dates = groups * dates_own
    bases, cols = lent_ref.shape[1:]
    block_rows = pixels // cols
    proj[...] = dot(gain_ref[:, :dates], pix_ref[:, 0].reshape(dates, pixels)) + dot(
        gain_ref[:, dates:], pix_ref[:, 1].reshape(dates, pixels)
    )
    below = [block_rows, block_rows + 1]
    above = [-2, -1]
    slots = [(0, r) for r in range(block_rows)] + [(1, r) for r in range(block_rows)]
    slots += [(0, r) for r in below] + [(1, r) for r in below]
    slots += [(1, r) for r in above] + [(0, r) for r in above]
    inner = 2 * block_rows
    sub = 8
    for k in range(0, bases, sub):
        for c in range(2):
            terms = [
                [
                    proj[
                        pl.ds((c * (REACH + 1) + j) * bases + k, sub),
                        pl.ds(row * cols, cols),
                    ]
                    for row in range(block_rows)
                ]
                for j in range(REACH + 1)
            ]
            for q, (part, row) in enumerate(slots):
                if part != c:
                    continue
                out = None
                for j in range(-REACH, REACH + 1):
                    if 0 <= row + j < block_rows:
                        term = terms[abs(j)][row + j]
                        out = term if out is None else out + term
                if q < inner:
                    stage[pl.ds(q * bases + k, sub), :] = out
                else:
                    lent_ref[q - inner, pl.ds(k, sub), :] = out
    own = bases // groups
    for d in range(groups):
        rows = [
            stage[pl.ds(c * block_rows * bases + d * own + k, block_rows, stride=bases), :]
            for k in range(own)
            for c in range(2)
        ]
        out_ref[d, : len(rows) * block_rows, :] = jnp.concatenate(rows, 0).astype(
            jnp.bfloat16
        )


def pack_kernel(part_ref, lent_ref, edge_ref, out_ref, held):
    del part_ref
    groups, height, _ = out_ref.shape
    slots, bases, _ = lent_ref.shape
    own = bases // groups
    opens = lax.axis_index("date") == 0
    closes = lax.axis_index("date") == groups - 1
    for i in range(slots):
        value = lent_ref[i]
        if i >= 2 * REACH:
            value = jnp.where(opens, edge_ref[i - 2 * REACH].astype(jnp.float32), value)
        else:
            value = jnp.where(closes, edge_ref[i].astype(jnp.float32), value)
        held[pl.ds(i * bases, bases), :] = value
    for d in range(groups):
        rows = [held[pl.ds(d * own + k, slots, stride=bases), :] for k in range(own)]
        out_ref[d, height - own * slots :, :] = jnp.concatenate(rows, 0).astype(jnp.bfloat16)


def join_kernel(part_ref, out_ref):
    groups = part_ref.shape[0]
    own, _, rows, cols = out_ref.shape
    block_rows = rows // groups
    sub = lax.broadcasted_iota(jnp.int32, (block_rows, cols), 0)
    base = own * 2 * block_rows
    for k in range(own):
        start = base + k * block_rows
        lends = [
            part_ref[b, start : start + block_rows, :].astype(jnp.float32)
            for b in range(groups)
        ]
        for b in range(groups):
            for c in range(2):
                start = (k * 2 + c) * block_rows
                main = part_ref[b, start : start + block_rows, :].astype(jnp.float32)
                before = lends[b - 1]
                after = lends[(b + 1) % groups]
                if c == 1:
                    before = pltpu.roll(before, block_rows - 2, 0)
                    after = pltpu.roll(after, 2, 0)
                out_ref[k, c, b * block_rows : (b + 1) * block_rows, :] = (
                    main
                    + jnp.where(sub < 2, before, 0.0)
                    + jnp.where(sub >= block_rows - 2, after, 0.0)
                )


def on_chip(x):
    return x if INTERPRET else pltpu.with_memory_space_constraint(x, pltpu.VMEM)


def chip_out(shape, dtype):
    return jax.ShapeDtypeStruct(shape, dtype) if INTERPRET else pltpu.VMEM(shape, dtype)


VMEM = pl.BlockSpec(memory_space=pltpu.VMEM)
ANY = pl.BlockSpec(memory_space=pl.ANY)
SMEM = pl.BlockSpec(memory_space=pltpu.SMEM)


def swaps(pairs):
    return [pair for a, b in pairs for pair in ((a, b), (b, a))]


def on_device(slc_stack, fir_taps, look_index, shrink_level, window_half, basis):
    date_local, rows, cols = slc_stack.shape[1:]
    groups = lax.axis_size("date")
    slabs = lax.axis_size("az")
    block_rows = rows // groups
    pixels = block_rows * cols
    bases, dates = basis.shape
    own = bases // groups

    rim_shape = (2, REACH, date_local, cols)
    small = (fir_taps.T, look_index.reshape(1, -1), window_half.reshape(1, dates), basis)
    fetched, near, far, taps, look, half, basis = pl.pallas_call(
        fetch_kernel,
        out_shape=(
            chip_out(slc_stack.shape, jnp.bfloat16),
            chip_out(rim_shape, jnp.bfloat16),
            chip_out(rim_shape, jnp.bfloat16),
        )
        + tuple(chip_out(x.shape, x.dtype) for x in small),
        in_specs=[ANY] * 5,
        out_specs=(VMEM,) * 7,
        scratch_shapes=[
            pltpu.VMEM((date_local * 16, cols), jnp.float32),
            pltpu.SemaphoreType.DMA((14,)),
        ],
        interpret=INTERPRET,
        name="fetch",
    )(slc_stack, *small)
    near = lax.ppermute(near, "az", swaps([(i, i + 1) for i in range(0, slabs - 1, 2)]))
    far = lax.ppermute(far, "az", swaps([(i, i + 1) for i in range(1, slabs - 1, 2)]))
    pitch = rows + 8
    shape = (groups, 2, date_local, pixels)
    blocks, rim, level = pl.pallas_call(
        filter_kernel,
        out_shape=(
            chip_out(shape, jnp.bfloat16),
            chip_out((2, 2, 2 * REACH, date_local, cols), jnp.float32),
            chip_out((1, cols), jnp.float32),
        ),
        in_specs=[VMEM, VMEM, SMEM],
        out_specs=(VMEM,) * 3,
        scratch_shapes=[pltpu.VMEM((date_local * pitch, cols), jnp.float32)],
        interpret=INTERPRET,
        name="azimuth_filter",
    )(on_chip(fetched), on_chip(taps), shrink_level)
    blocks = pl.pallas_call(
        rim_kernel,
        out_shape=chip_out(shape, jnp.bfloat16),
        in_specs=[VMEM] * 5,
        out_specs=VMEM,
        input_output_aliases={0: 0},
        interpret=INTERPRET,
        name="filter_rim",
    )(on_chip(blocks), on_chip(rim), on_chip(near), on_chip(far), on_chip(taps))
    pix = lax.all_to_all(blocks, "date", split_axis=0, concat_axis=0, tiled=True)

    pix = on_chip(pix)
    rows_all = 2 * (REACH + 1) * bases
    gain, edge = pl.pallas_call(
        link_kernel,
        out_shape=(
            chip_out((rows_all, 2 * dates), jnp.bfloat16),
            chip_out((2 * REACH, bases, cols), jnp.bfloat16),
        ),
        in_specs=[VMEM] * 5,
        out_specs=(VMEM, VMEM),
        interpret=INTERPRET,
        name="phase_link",
    )(pix, on_chip(look), on_chip(level), on_chip(half), on_chip(basis))
    edge = lax.ppermute(
        edge,
        ("date", "az"),
        [((groups - 1) * slabs + a, (groups - 1) * slabs + a + 1) for a in range(slabs - 1)]
        + [(a + 1, a) for a in range(slabs - 1)],
    )
    packed = (groups, 3 * own * block_rows, cols)
    own_rows, lent = pl.pallas_call(
        project_kernel,
        out_shape=(
            chip_out(packed, jnp.bfloat16),
            chip_out((4 * REACH, bases, cols), jnp.float32),
        ),
        in_specs=[VMEM, VMEM],
        out_specs=(VMEM, VMEM),
        scratch_shapes=[
            pltpu.VMEM((rows_all, pixels), jnp.float32),
            pltpu.VMEM((2 * block_rows * bases, cols), jnp.float32),
        ],
        interpret=INTERPRET,
        name="project",
    )(pix, on_chip(gain))
    lent = pl.pallas_call(
        pack_kernel,
        out_shape=chip_out(packed, jnp.bfloat16),
        in_specs=[VMEM] * 3,
        out_specs=VMEM,
        scratch_shapes=[pltpu.VMEM((4 * REACH * bases, cols), jnp.float32)],
        input_output_aliases={0: 0},
        interpret=INTERPRET,
        name="pack_rows",
    )(on_chip(own_rows), on_chip(lent), on_chip(edge))
    parts = lax.all_to_all(lent, "date", split_axis=0, concat_axis=0, tiled=True)
    return pl.pallas_call(
        join_kernel,
        out_shape=jax.ShapeDtypeStruct((own, 2, rows, cols), jnp.float32),
        in_specs=[VMEM],
        out_specs=VMEM,
        interpret=INTERPRET,
        name="overlap_add",
    )(on_chip(parts))


def solution(mesh):
    in_specs = (
        P(None, "date", "az", None),
        P("date", None),
        P("az", "date", None),
        P("az", "date"),
        P(),
        P(),
    )
    out_specs = P("date", None, "az", None)
    return jax.shard_map(
        on_device, mesh=mesh, in_specs=in_specs, out_specs=out_specs, check_vma=False
    )
```

```python
import jax
import jax.numpy as jnp
from jax import lax
from jax.experimental import pallas as pl
from jax.experimental.pallas import tpu as pltpu
from jax.sharding import PartitionSpec as P


NS_ITERS = 6
REACH = 2
INTERPRET = False


def spread(taps_ref, cols):
    columns = taps_ref[...].T
    return [
        jnp.broadcast_to(columns[:, j : j + 1], (columns.shape[0], cols))
        for j in range(2 * REACH + 1)
    ]


def weigh(taps, window):
    total = taps[0] * window[0]
    for j in range(1, 2 * REACH + 1):
        total = total + taps[j] * window[j]
    return total.astype(jnp.bfloat16)


def fetch_kernel(
    slc_hbm,
    taps_hbm,
    look_hbm,
    half_hbm,
    basis_hbm,
    slc_ref,
    near_ref,
    far_ref,
    taps_ref,
    look_ref,
    half_ref,
    basis_ref,
    held,
    sems,
):
    _, dates, rows, _ = slc_ref.shape
    tile = held.shape[0] // dates
    parts = 4
    share = dates // parts
    spans = [(pl.ds(0, 2), pl.ds(0, dates), 0, tile)]
    spans += [(pl.ds(0, 2), pl.ds(0, dates), rows - tile, tile)]
    spans += [
        (pl.ds(c, 1), pl.ds(i * share, share), tile, rows - 2 * tile)
        for c in range(2)
        for i in range(parts)
    ]
    loads = [
        pltpu.make_async_copy(
            slc_hbm.at[c, t, pl.ds(start, size), :],
            slc_ref.at[c, t, pl.ds(start, size), :],
            sems.at[i],
        )
        for i, (c, t, start, size) in enumerate(spans)
    ]
    small = [
        (taps_hbm, taps_ref),
        (look_hbm, look_ref),
        (half_hbm, half_ref),
        (basis_hbm, basis_ref),
    ]
    loads += [
        pltpu.make_async_copy(a, b, sems.at[len(spans) + i])
        for i, (a, b) in enumerate(small)
    ]
    for load in loads:
        load.start()
    even = (lax.axis_index("az") & 1) == 0
    loads[0].wait()
    loads[1].wait()
    for c in range(2):
        edges = []
        for start, row in ((0, 0), (rows - tile, tile - REACH)):
            for t in range(dates):
                held[pl.ds(t * tile, tile), :] = slc_ref[
                    c, t, pl.ds(start, tile), :
                ].astype(jnp.float32)
            edges.append(
                [held[pl.ds(row + i, dates, stride=tile), :] for i in range(REACH)]
            )
        for i in range(REACH):
            first, last = edges[0][i], edges[1][i]
            near_ref[c, i] = jnp.where(even, last, first).astype(jnp.bfloat16)
            far_ref[c, i] = jnp.where(even, first, last).astype(jnp.bfloat16)
    for load in loads[2:]:
        load.wait()


def filter_kernel(slc_ref, taps_ref, level_smem, out_ref, rim_ref, level_ref, held):
    _, dates, rows, cols = slc_ref.shape
    blocks = out_ref.shape[0]
    block_rows = rows // blocks
    pitch = held.shape[0] // dates
    taps = spread(taps_ref, cols)
    level_ref[...] = jnp.full(level_ref.shape, level_smem[0, 0].astype(jnp.float32))
    for c in range(2):
        for t in range(dates):
            held[pl.ds(t * pitch, rows), :] = slc_ref[c, t].astype(jnp.float32)

        def line(r):
            return held[pl.ds(r, dates, stride=pitch), :]

        window = [line(r) for r in range(2 * REACH)]
        for i in range(2 * REACH):
            rim_ref[0, c, i] = window[i]
        for r in range(REACH, rows - REACH):
            window.append(line(r + REACH))
            b, i = divmod(r, block_rows)
            out_ref[b, c, :, i * cols : (i + 1) * cols] = weigh(taps, window)
            window.pop(0)
        for i in range(2 * REACH):
            rim_ref[1, c, i] = window[i]


def rim_kernel(part_ref, rim_ref, near_ref, far_ref, taps_ref, out_ref):
    del part_ref
    blocks = out_ref.shape[0]
    cols = rim_ref.shape[-1]
    block_rows = out_ref.shape[-1] // cols
    even = (lax.axis_index("az") & 1) == 0
    taps = spread(taps_ref, cols)
    for c in range(2):
        own = [[rim_ref[side, c, i] for i in range(2 * REACH)] for side in range(2)]
        near = [near_ref[c, i].astype(jnp.float32) for i in range(REACH)]
        far = [far_ref[c, i].astype(jnp.float32) for i in range(REACH)]
        low = [jnp.where(even, b, a) for a, b in zip(near, far)] + own[0]
        high = own[1] + [jnp.where(even, a, b) for a, b in zip(near, far)]
        for i in range(REACH):
            window = slice(i, i + 2 * REACH + 1)
            out_ref[0, c, :, i * cols : (i + 1) * cols] = weigh(taps, low[window])
            row = block_rows - REACH + i
            out_ref[blocks - 1, c, :, row * cols : (row + 1) * cols] = weigh(
                taps, high[window]
            )


def split(x):
    hi = x.astype(jnp.bfloat16)
    return hi, (x - hi.astype(jnp.float32)).astype(jnp.bfloat16)


def dot(a, b):
    return jnp.dot(a, b, preferred_element_type=jnp.float32)


def dot3(a, b):
    a_hi, a_lo = split(a)
    b_hi, b_lo = split(b)
    return dot(
        jnp.concatenate([a_hi, a_lo, a_hi], 1), jnp.concatenate([b_hi, b_hi, b_lo], 0)
    )


def total(x):
    return jnp.sum(jnp.sum(x, axis=1, keepdims=True), axis=0, keepdims=True)


def link_kernel(
    pix_ref, look_ref, level_ref, half_ref, basis_ref, gain_ref, edge_ref
):
    groups, _, dates_own, pixels = pix_ref.shape
    dates = groups * dates_own
    looks = look_ref.shape[1]
    width = 2 * looks
    bases = basis_ref.shape[0]
    cols = edge_ref.shape[2]
    place = lax.broadcasted_iota(jnp.int32, (pixels, width), 0)
    chosen = jnp.concatenate([look_ref[...], look_ref[...]], 1)
    picked = (place == chosen).astype(jnp.float32).astype(jnp.bfloat16)
    samp_re = dot(pix_ref[:, 0].reshape(dates, pixels), picked)
    samp_im = dot(pix_ref[:, 1].reshape(dates, pixels), picked)
    first = lax.broadcasted_iota(jnp.int32, (dates, width), 1) < looks
    tall = jnp.concatenate(
        [jnp.where(first, samp_re, -samp_im), jnp.where(first, samp_im, samp_re)], 0
    )
    wide = tall.T.astype(jnp.bfloat16)
    tall = tall.astype(jnp.bfloat16)
    inner = dot(wide[:looks], tall)

    half = half_ref[...]
    share = basis_ref[...].astype(jnp.float32) / (2 * half + 1).astype(jnp.float32)
    near = jnp.concatenate(
        [jnp.where(half >= j, share, 0.0) for j in range(REACH + 1)], axis=0
    )
    near_hi, near_lo = split(near)
    seen = dot(near_hi, tall[:dates]) + dot(near_lo, tall[:dates])

    cols_i = lax.broadcasted_iota(jnp.int32, (looks, width), 1)
    turn = jnp.where(cols_i < looks, -1.0, 1.0)

    def whole(top):
        return jnp.concatenate([top, turn * pltpu.roll(top, looks, 1)], 0)

    trace = total(samp_re * samp_re + samp_im * samp_im) * 0.5
    square = total(inner * inner)
    mean = trace / (looks * dates) + 1e-06
    weight = level_ref[:, :1] / 16.0
    alpha = weight * mean + mean
    beta = (1.0 - weight) / looks
    scale = 1.0 / jnp.sqrt(
        dates * alpha * alpha + 2.0 * alpha * beta * trace + beta * beta * square
    )

    t = scale * alpha
    x = jnp.ones_like(t)
    w = (scale * beta) * inner
    full = whole(w)
    m = (2.0 - 2.0 * t) * seen - dot3(seen, full)
    u = -seen
    w = (2.0 - 2.0 * t) * w - dot3(w, full)
    x, t = x * (2.0 - t), 2.0 * t - t * t
    for step in range(1, NS_ITERS):
        full = whole(w)
        if step < NS_ITERS - 1:
            w = (2.0 - 2.0 * t) * w - dot3(w, full)
        prod = dot3(jnp.concatenate([m, u], 0), full)
        m, u = (
            (2.0 - 2.0 * t) * m - prod[: m.shape[0]],
            (2.0 - t) * u - x * m - prod[m.shape[0] :],
        )
        x, t = x * (2.0 - t), 2.0 * t - t * t

    core = (scale * beta) * (m - (mean * scale) * u)
    core_hi, core_lo = split(core)
    gain = dot(core_hi, wide) + dot(core_lo, wide)
    plain = (t - mean * scale * x) * near
    left = gain[:, :dates] + plain
    right = gain[:, dates:]
    gain_re = jnp.concatenate([left, -right], 0).astype(jnp.bfloat16)
    gain_im = jnp.concatenate([right, left], 0).astype(jnp.bfloat16)
    gain_ref[:, :dates] = gain_re
    gain_ref[:, dates:] = gain_im

    opens = lax.axis_index("date") == 0
    side = pl.multiple_of(jnp.where(opens, 0, pixels - REACH * cols), cols)
    outer = [
        pix_ref[:, c, :, pl.ds(side, REACH * cols)].reshape(dates, REACH * cols)
        for c in range(2)
    ]
    rows = (REACH + 1) * bases
    tops, bottoms = {}, {}
    for c in range(2):
        lines = slice(c * rows + bases, (c + 1) * rows)
        proj = dot(gain_re[lines], outer[0]) + dot(gain_im[lines], outer[1])

        def part(j, row):
            return proj[(j - 1) * bases : j * bases, row * cols : (row + 1) * cols]

        above = [part(2, 0), part(1, 0) + part(2, 1)]
        below = [part(2, 0) + part(1, 1), part(2, 1)]
        tops[c] = above
        bottoms[c] = below
    up = tops[1] + tops[0]
    down = bottoms[0] + bottoms[1]
    for i in range(2 * REACH):
        edge_ref[i] = jnp.where(opens, up[i], down[i]).astype(jnp.bfloat16)


def project_kernel(pix_ref, gain_ref, out_ref, lent_ref, proj, stage):
    groups, _, dates_own, pixels = pix_ref.shape
    dates = groups * dates_own
    bases, cols = lent_ref.shape[1:]
    block_rows = pixels // cols
    proj[...] = dot(gain_ref[:, :dates], pix_ref[:, 0].reshape(dates, pixels)) + dot(
        gain_ref[:, dates:], pix_ref[:, 1].reshape(dates, pixels)
    )
    below = [block_rows, block_rows + 1]
    above = [-2, -1]
    slots = [(0, r) for r in range(block_rows)] + [(1, r) for r in range(block_rows)]
    slots += [(0, r) for r in below] + [(1, r) for r in below]
    slots += [(1, r) for r in above] + [(0, r) for r in above]
    inner = 2 * block_rows
    sub = 8
    for k in range(0, bases, sub):
        for c in range(2):
            terms = [
                [
                    proj[
                        pl.ds((c * (REACH + 1) + j) * bases + k, sub),
                        pl.ds(row * cols, cols),
                    ]
                    for row in range(block_rows)
                ]
                for j in range(REACH + 1)
            ]
            for q, (part, row) in enumerate(slots):
                if part != c:
                    continue
                out = None
                for j in range(-REACH, REACH + 1):
                    if 0 <= row + j < block_rows:
                        term = terms[abs(j)][row + j]
                        out = term if out is None else out + term
                if q < inner:
                    stage[pl.ds(q * bases + k, sub), :] = out
                else:
                    lent_ref[q - inner, pl.ds(k, sub), :] = out
    own = bases // groups
    for d in range(groups):
        rows = [
            stage[pl.ds(c * block_rows * bases + d * own + k, block_rows, stride=bases), :]
            for k in range(own)
            for c in range(2)
        ]
        out_ref[d, : len(rows) * block_rows, :] = jnp.concatenate(rows, 0).astype(
            jnp.bfloat16
        )


def pack_kernel(part_ref, lent_ref, edge_ref, out_ref, held):
    del part_ref
    groups, height, _ = out_ref.shape
    slots, bases, _ = lent_ref.shape
    own = bases // groups
    opens = lax.axis_index("date") == 0
    closes = lax.axis_index("date") == groups - 1
    for i in range(slots):
        value = lent_ref[i]
        if i >= 2 * REACH:
            value = jnp.where(opens, edge_ref[i - 2 * REACH].astype(jnp.float32), value)
        else:
            value = jnp.where(closes, edge_ref[i].astype(jnp.float32), value)
        held[pl.ds(i * bases, bases), :] = value
    for d in range(groups):
        rows = [held[pl.ds(d * own + k, slots, stride=bases), :] for k in range(own)]
        out_ref[d, height - own * slots :, :] = jnp.concatenate(rows, 0).astype(jnp.bfloat16)


def join_kernel(part_ref, out_ref):
    groups = part_ref.shape[0]
    own, _, rows, cols = out_ref.shape
    block_rows = rows // groups
    sub = lax.broadcasted_iota(jnp.int32, (block_rows, cols), 0)
    base = own * 2 * block_rows
    for k in range(own):
        start = base + k * block_rows
        lends = [
            part_ref[b, start : start + block_rows, :].astype(jnp.float32)
            for b in range(groups)
        ]
        for b in range(groups):
            for c in range(2):
                start = (k * 2 + c) * block_rows
                main = part_ref[b, start : start + block_rows, :].astype(jnp.float32)
                before = lends[b - 1]
                after = lends[(b + 1) % groups]
                if c == 1:
                    before = pltpu.roll(before, block_rows - 2, 0)
                    after = pltpu.roll(after, 2, 0)
                out_ref[k, c, b * block_rows : (b + 1) * block_rows, :] = (
                    main
                    + jnp.where(sub < 2, before, 0.0)
                    + jnp.where(sub >= block_rows - 2, after, 0.0)
                )


def on_chip(x):
    return x if INTERPRET else pltpu.with_memory_space_constraint(x, pltpu.VMEM)


def chip_out(shape, dtype):
    return jax.ShapeDtypeStruct(shape, dtype) if INTERPRET else pltpu.VMEM(shape, dtype)


VMEM = pl.BlockSpec(memory_space=pltpu.VMEM)
ANY = pl.BlockSpec(memory_space=pl.ANY)
SMEM = pl.BlockSpec(memory_space=pltpu.SMEM)


def swaps(pairs):
    return [pair for a, b in pairs for pair in ((a, b), (b, a))]


def on_device(slc_stack, fir_taps, look_index, shrink_level, window_half, basis):
    date_local, rows, cols = slc_stack.shape[1:]
    groups = lax.axis_size("date")
    slabs = lax.axis_size("az")
    block_rows = rows // groups
    pixels = block_rows * cols
    bases, dates = basis.shape
    own = bases // groups

    rim_shape = (2, REACH, date_local, cols)
    small = (fir_taps.T, look_index.reshape(1, -1), window_half.reshape(1, dates), basis)
    fetched, near, far, taps, look, half, basis = pl.pallas_call(
        fetch_kernel,
        out_shape=(
            chip_out(slc_stack.shape, jnp.bfloat16),
            chip_out(rim_shape, jnp.bfloat16),
            chip_out(rim_shape, jnp.bfloat16),
        )
        + tuple(chip_out(x.shape, x.dtype) for x in small),
        in_specs=[ANY] * 5,
        out_specs=(VMEM,) * 7,
        scratch_shapes=[
            pltpu.VMEM((date_local * 16, cols), jnp.float32),
            pltpu.SemaphoreType.DMA((14,)),
        ],
        interpret=INTERPRET,
        name="fetch",
    )(slc_stack, *small)
    near = lax.ppermute(near, "az", swaps([(i, i + 1) for i in range(0, slabs - 1, 2)]))
    far = lax.ppermute(far, "az", swaps([(i, i + 1) for i in range(1, slabs - 1, 2)]))
    pitch = rows + 8
    shape = (groups, 2, date_local, pixels)
    blocks, rim, level = pl.pallas_call(
        filter_kernel,
        out_shape=(
            chip_out(shape, jnp.bfloat16),
            chip_out((2, 2, 2 * REACH, date_local, cols), jnp.float32),
            chip_out((1, cols), jnp.float32),
        ),
        in_specs=[VMEM, VMEM, SMEM],
        out_specs=(VMEM,) * 3,
        scratch_shapes=[pltpu.VMEM((date_local * pitch, cols), jnp.float32)],
        interpret=INTERPRET,
        name="azimuth_filter",
    )(on_chip(fetched), on_chip(taps), shrink_level)
    blocks = pl.pallas_call(
        rim_kernel,
        out_shape=chip_out(shape, jnp.bfloat16),
        in_specs=[VMEM] * 5,
        out_specs=VMEM,
        input_output_aliases={0: 0},
        interpret=INTERPRET,
        name="filter_rim",
    )(on_chip(blocks), on_chip(rim), on_chip(near), on_chip(far), on_chip(taps))
    pix = lax.all_to_all(blocks, "date", split_axis=0, concat_axis=0, tiled=True)

    pix = on_chip(pix)
    rows_all = 2 * (REACH + 1) * bases
    gain, edge = pl.pallas_call(
        link_kernel,
        out_shape=(
            chip_out((rows_all, 2 * dates), jnp.bfloat16),
            chip_out((2 * REACH, bases, cols), jnp.bfloat16),
        ),
        in_specs=[VMEM] * 5,
        out_specs=(VMEM, VMEM),
        interpret=INTERPRET,
        name="phase_link",
    )(pix, on_chip(look), on_chip(level), on_chip(half), on_chip(basis))
    edge = lax.ppermute(
        edge,
        ("date", "az"),
        [((groups - 1) * slabs + a, (groups - 1) * slabs + a + 1) for a in range(slabs - 1)]
        + [(a + 1, a) for a in range(slabs - 1)],
    )
    packed = (groups, 3 * own * block_rows, cols)
    own_rows, lent = pl.pallas_call(
        project_kernel,
        out_shape=(
            chip_out(packed, jnp.bfloat16),
            chip_out((4 * REACH, bases, cols), jnp.float32),
        ),
        in_specs=[VMEM, VMEM],
        out_specs=(VMEM, VMEM),
        scratch_shapes=[
            pltpu.VMEM((rows_all, pixels), jnp.float32),
            pltpu.VMEM((2 * block_rows * bases, cols), jnp.float32),
        ],
        interpret=INTERPRET,
        name="project",
    )(pix, on_chip(gain))
    lent = pl.pallas_call(
        pack_kernel,
        out_shape=chip_out(packed, jnp.bfloat16),
        in_specs=[VMEM] * 3,
        out_specs=VMEM,
        scratch_shapes=[pltpu.VMEM((4 * REACH * bases, cols), jnp.float32)],
        input_output_aliases={0: 0},
        interpret=INTERPRET,
        name="pack_rows",
    )(on_chip(own_rows), on_chip(lent), on_chip(edge))
    parts = lax.all_to_all(lent, "date", split_axis=0, concat_axis=0, tiled=True)
    return pl.pallas_call(
        join_kernel,
        out_shape=jax.ShapeDtypeStruct((own, 2, rows, cols), jnp.float32),
        in_specs=[VMEM],
        out_specs=VMEM,
        interpret=INTERPRET,
        name="overlap_add",
    )(on_chip(parts))


def solution(mesh):
    in_specs = (
        P(None, "date", "az", None),
        P("date", None),
        P("az", "date", None),
        P("az", "date"),
        P(),
        P(),
    )
    out_specs = P("date", None, "az", None)
    return jax.shard_map(
        on_device, mesh=mesh, in_specs=in_specs, out_specs=out_specs, check_vma=False
    )
```
